512 devices in a mesh: dp: 4 (over x), ctx: 32 (over z, core), tp: 4 (over y).
Axes of the slice: x: 4, y: 4, z: 16, core: 2. Of those that a mesh axis runs over, the one named last changes fastest.
Arguments:
- inputs: bfloat16 [4, 4096, 8192], P('dp', 'ctx', 'tp'), may hold values from -6 to 6
- grad_out: bfloat16 [4, 4096, 8192], P('dp', 'ctx', 'tp'), may hold values from -6 to 6
- input_map: bfloat16 [4, 4096, 128], P('dp', 'ctx'), may hold values from -0.5 to 0.5
- output_map: bfloat16 [4, 4096, 128], P('dp', 'ctx'), may hold values from -0.25 to 0.25
- step_size: float32 [4, 128, 4096], P('dp', 'tp', 'ctx'), may hold values from 0.3 to 1.5
- log_decay: float32 [4, 128, 4096], P('dp', 'tp', 'ctx'), may hold values from -2 to 0
- skip_gain: float32 [128], P('tp'), may hold values from 0.5 to 1.5
Outputs:
- mixed: bfloat16 [4, 4096, 8192], P('dp', 'ctx', 'tp')
- grad_inputs: bfloat16 [4, 4096, 8192], P('dp', 'ctx', 'tp')
- grad_step: float32 [4, 128, 4096], P('dp', 'tp', 'ctx')
- grad_decay: float32 [4, 128, 4096], P('dp', 'tp', 'ctx')
- grad_input_map: float32 [4, 4096, 128], P('dp', ('ctx', 'tp'))
- grad_output_map: float32 [4, 4096, 128], P('dp', ('ctx', 'tp'))
- grad_skip: float32 [128], P('tp')
The draws below stay inside these ranges and needn't reach their ends.
All inputs are finite; a program needn't handle non-finite values.
Results may differ from the reference program's by a relative error of at most 0.0011.
Values sent between devices are 32-bit elements; how exact they have to be, the bound alone decides.
No kernel may reach another device: no remote copies, remote signals or barrier semaphores. Data moves between devices by JAX's collectives and lax.ppermute only.
A program may use at most 192 MiB of HBM per device.

```python
import math
import jax
import jax.numpy as jnp
from jax import lax

H = 128
P_SIZE = 64
N = 128
TOK_DEV = 128
BATCH = 4
SEQ = 4096
HP = 8192


def draw_log_decay(key, part):
    keys = jax.random.split(key, 7)
    slow_heads = jax.random.bernoulli(keys[0], 0.5, (H,))
    approximate_guess = jnp.exp(jax.random.uniform(keys[3], (BATCH, H, SEQ), minval=math.log(0.5), maxval=math.log(2.0)))
    slow_rate = jax.random.uniform(keys[1], (H,), minval=0.12, maxval=0.4) / SEQ
    fast_rate = jnp.exp(jax.random.uniform(keys[2], (H,), minval=math.log(1.0 / 50.0), maxval=math.log(1.0 / 30.0)))
    fading_speeds = jnp.where(slow_heads, slow_rate, fast_rate)
    slab_count = SEQ // TOK_DEV
    block_scaling_factor = jnp.exp(jax.random.uniform(keys[4], (BATCH, 1, slab_count), minval=math.log(0.6), maxval=math.log(1.8)))
    block_scaling_factor = jnp.repeat(block_scaling_factor, TOK_DEV, axis=2)
    location_cells = jax.random.randint(keys[5], (BATCH, 3), 0, SEQ)
    layering_tiers = jax.random.uniform(keys[6], (BATCH, 3), minval=0.22, maxval=0.45)
    word_indices = jnp.arange(SEQ, dtype=jnp.int32)
    cluster_partition = jnp.sum(jnp.where(word_indices[None, None, :] == location_cells[:, :, None], layering_tiers[:, :, None], 0.0), axis=1)
    return -(fading_speeds[None, :, None] * approximate_guess * block_scaling_factor) - cluster_partition[:, None, :]


def levels(stream_key, dims, cuts, least, top_value):
    def one(axis_at, parts):
        draws = jax.random.uniform(jax.random.fold_in(jax.random.fold_in(stream_key, 6), axis_at), (parts,), jnp.float32, least / len(cuts), top_value / len(cuts))
        return jnp.repeat(jnp.exp(draws), dims[axis_at] // parts).reshape((-1,) + (1,) * (len(dims) - axis_at - 1))

    gain = one(*cuts[0])
    for cut in cuts[1:]:
        gain = gain * one(*cut)
    return gain


def normal_values(own_key, dims, width, limit, cuts=(), kind=jnp.bfloat16):
    result = jax.random.normal(own_key, dims, jnp.float32) * width
    if len(cuts) > 0:
        result = levels(own_key, dims, cuts, -0.22, 0.18) * result
    return jnp.clip(result, min=-limit, max=limit).astype(kind)


def setup_inputs(seed: int = 0) -> dict:
    key_of = jax.random.split(jax.random.key(seed), 8)
    return {
        "inputs": normal_values(key_of[0], (BATCH, SEQ, HP), 1.0, 6.0, ((0, 4), (1, 32), (2, 4))),
        "grad_out": normal_values(key_of[1], (BATCH, SEQ, HP), 1.0, 6.0, ((0, 4), (1, 32), (2, 4))),
        "input_map": normal_values(key_of[2], (BATCH, SEQ, N), N ** -0.5, 0.5, ((0, 4), (1, 32))),
        "output_map": normal_values(key_of[3], (BATCH, SEQ, N), (SEQ ** -0.5), 0.25, ((0, 4), (1, 32))),
        "step_size": jnp.clip(jnp.exp(math.log(1.5) - 1.60943787 * jax.random.uniform(key_of[4], (BATCH, H, SEQ), jnp.float32) ** levels(key_of[4], (BATCH, H, SEQ), ((0, 4), (1, 4), (2, 32)), -0.2, 0.2)), 0.3, 1.5),
        "log_decay": draw_log_decay(jax.random.fold_in(key_of[7], 71), 0),
        "skip_gain": jnp.clip(0.5 + 1.0 * jax.random.uniform(key_of[6], (H,), jnp.float32) ** levels(key_of[6], (H,), ((0, 4),), -0.2, 0.2), 0.5, 1.5),
    }


precise = lax.Precision.HIGHEST

def block_forward(values, in_map, out_map, steps, logs):
    cumulative = jnp.cumsum(logs, axis=-1)
    length = cumulative.shape[-1]
    row_ids = lax.broadcasted_iota(jnp.int32, (length, length), 0)
    column_ids = lax.broadcasted_iota(jnp.int32, (length, length), 1)
    causal = row_ids >= column_ids
    spread = cumulative[..., :, None] - cumulative[..., None, :]
    decays = jnp.where(causal, jnp.exp(jnp.where(causal, spread, 0.0)), 0.0)
    affinity = jnp.einsum('btn,bsn->bts', out_map, in_map, precision=precise)
    mixing = decays * affinity[:, None]
    scaled = values * jnp.transpose(steps, (0, 2, 1))[..., None]
    remain = jnp.exp(cumulative[..., -1:] - cumulative)
    weighted = remain[..., None] * in_map[:, None]
    local_state = jnp.einsum('bshp,bhsn->bhpn', scaled, weighted, precision=precise)
    through = jnp.exp(cumulative[..., -1])
    return (cumulative, decays, mixing, scaled, remain, local_state, through)

def block_output(values, out_map, skip_gain, cumulative, mixing, scaled, incoming):
    within = jnp.einsum('bhts,bshp->bthp', mixing, scaled, precision=precise)
    carried = jnp.einsum('bhpn,btn->bthp', incoming, out_map, precision=precise)
    carried = carried * jnp.transpose(jnp.exp(cumulative), (0, 2, 1))[..., None]
    return (within + carried + skip_gain[:, None] * values, carried)

def block_source(cotangent, out_map, cumulative):
    weighted = jnp.exp(cumulative)[..., None] * out_map[:, None]
    return jnp.einsum('bshp,bhsn->bhpn', cotangent, weighted, precision=precise)

def block_backward(values, cotangent, in_map, out_map, steps, skip_gain, cumulative, decays, mixing, scaled, remain, local_state, through, incoming, carried, arriving):
    remain_col = jnp.transpose(remain, (0, 2, 1))[..., None]
    starts = jnp.transpose(jnp.exp(cumulative), (0, 2, 1))[..., None]
    steps_col = jnp.transpose(steps, (0, 2, 1))[..., None]
    from_later = jnp.einsum('bhpn,btn->bthp', arriving, in_map, precision=precise)
    state_grad = jnp.einsum('bhst,bshp->bthp', mixing, cotangent, precision=precise) + remain_col * from_later
    grad_values = steps_col * state_grad + skip_gain[:, None] * cotangent
    grad_steps = jnp.transpose(lax.optimization_barrier(jnp.sum(values * state_grad, axis=-1)), (0, 2, 1))
    products = jnp.einsum('bthp,bshp->bhts', cotangent, scaled, precision=precise)
    summed = lax.optimization_barrier(jnp.sum(decays * products, axis=1))
    grad_in_map = jnp.einsum('bts,btn->bsn', summed, out_map, precision=precise) + jnp.einsum('bthp,bhpn->btn', scaled * remain_col, arriving, precision=precise)
    grad_out_map = jnp.einsum('bts,bsn->btn', summed, in_map, precision=precise) + jnp.einsum('bthp,bhpn->btn', cotangent * starts, incoming, precision=precise)
    paired = mixing * products
    change = lax.optimization_barrier(jnp.sum(paired, axis=-1)) - lax.optimization_barrier(jnp.sum(paired, axis=-2))
    change = change + jnp.transpose(lax.optimization_barrier(jnp.sum(cotangent * carried, axis=-1)), (0, 2, 1))
    change = change - remain * jnp.transpose(lax.optimization_barrier(jnp.sum(scaled * from_later, axis=-1)), (0, 2, 1))
    final_edge = lax.optimization_barrier(jnp.sum(arriving * local_state, axis=(2, 3))) + through * lax.optimization_barrier(jnp.sum(arriving * incoming, axis=(2, 3)))
    length = change.shape[-1]
    ending = lax.broadcasted_iota(jnp.int32, (length,), 0) == length - 1
    change = change + jnp.where(ending, final_edge[..., None], 0.0)
    grad_logs = lax.cumsum(change, axis=2, reverse=True)
    skip_part = lax.optimization_barrier(jnp.sum(cotangent * values, axis=(0, 1, 3)))
    return (grad_values, grad_steps, grad_in_map, grad_out_map, grad_logs, skip_part)

def reference(inputs, grad_out, input_map, output_map, step_size, log_decay, skip_gain):
    sequences = inputs.shape[0]
    block_len = math.gcd(SEQ, 256)
    block_count = SEQ // block_len

    def by_tokens(tensor, trailing):
        return jnp.swapaxes(tensor.reshape((sequences, block_count, block_len) + trailing), 0, 1)

    def by_heads(tensor):
        return jnp.transpose(tensor.reshape(sequences, H, block_count, block_len), (2, 0, 1, 3))
    all_values = by_tokens(inputs, (H, P_SIZE))
    all_grads = by_tokens(grad_out, (H, P_SIZE))
    all_in = by_tokens(input_map, (N,))
    all_out = by_tokens(output_map, (N,))
    all_steps = by_heads(step_size)
    all_logs = by_heads(log_decay)
    empty_state = jnp.zeros((sequences, H, P_SIZE, N), jnp.float32)

    def forward(carry_state, pieces):
        part_values, part_in, part_out, part_steps, part_logs = pieces
        values = part_values.astype(jnp.float32)
        in_map = part_in.astype(jnp.float32)
        out_map = part_out.astype(jnp.float32)
        cumulative, decays, mixing, scaled, remain, local_state, through = block_forward(values, in_map, out_map, part_steps, part_logs)
        mixed, carried = block_output(values, out_map, skip_gain, cumulative, mixing, scaled, carry_state)
        return (through[..., None, None] * carry_state + local_state, (mixed.astype(jnp.bfloat16), carry_state))
    unused, (mixed_blocks, incomings) = lax.scan(forward, empty_state, (all_values, all_in, all_out, all_steps, all_logs))

    def backward(arriving, pieces):
        part_values, part_grads, part_in, part_out, part_steps, part_logs, incoming = pieces
        values = part_values.astype(jnp.float32)
        cotangent = part_grads.astype(jnp.float32)
        in_map = part_in.astype(jnp.float32)
        out_map = part_out.astype(jnp.float32)
        cumulative, decays, mixing, scaled, remain, local_state, through = block_forward(values, in_map, out_map, part_steps, part_logs)
        mixed, carried = block_output(values, out_map, skip_gain, cumulative, mixing, scaled, incoming)
        source = block_source(cotangent, out_map, cumulative)
        results = block_backward(values, cotangent, in_map, out_map, part_steps, skip_gain, cumulative, decays, mixing, scaled, remain, local_state, through, incoming, carried, arriving)
        return (source + through[..., None, None] * arriving, results)
    unused_back, results = lax.scan(backward, empty_state, (all_values, all_grads, all_in, all_out, all_steps, all_logs, incomings), reverse=True)
    grad_values, grad_steps, grad_in, grad_out_map, grad_logs, skip_parts = results
    mixed = jnp.swapaxes(mixed_blocks, 0, 1).reshape(sequences, SEQ, H * P_SIZE)
    grad_inputs = jnp.swapaxes(grad_values, 0, 1).reshape(sequences, SEQ, H * P_SIZE).astype(jnp.bfloat16)
    grad_step = jnp.transpose(grad_steps, (1, 2, 0, 3)).reshape(sequences, H, SEQ)
    grad_decay = jnp.transpose(grad_logs, (1, 2, 0, 3)).reshape(sequences, H, SEQ)
    grad_input_map = jnp.swapaxes(grad_in, 0, 1).reshape(sequences, SEQ, N)
    grad_output_map = jnp.swapaxes(grad_out_map, 0, 1).reshape(sequences, SEQ, N)
    grad_skip = lax.optimization_barrier(jnp.sum(skip_parts, axis=0)) / math.sqrt(sequences * SEQ * P_SIZE)
    return (mixed, grad_inputs, grad_step, grad_decay, grad_input_map, grad_output_map, grad_skip)
```

```python
import math

import jax
import jax.numpy as jnp
from jax import lax
from jax.experimental import pallas as pl
from jax.experimental.pallas import tpu as pltpu
from jax.sharding import PartitionSpec as P

F32 = jnp.float32
BF16 = jnp.bfloat16
HIGHEST = lax.Precision.HIGHEST
TOK = 128
HEADS = 32
PH = 64
NS = 128
QH = 8
QR = QH * PH
VMEM_LIMIT = 48 * 1024 * 1024


def iota(shape, dim):
    return lax.broadcasted_iota(jnp.int32, shape, dim)


def split(value):
    high = value.astype(BF16)
    low = (value - high.astype(F32)).astype(BF16)
    return high, low


def dot(a, b, ca, cb, precision=None):
    return lax.dot_general(a, b, (((ca,), (cb,)), ((), ())), preferred_element_type=F32, precision=precision)


def running_sum(logs):
    upto = (iota((TOK, TOK), 0) <= iota((TOK, TOK), 1)).astype(F32)
    return dot(logs, upto, 1, 0, HIGHEST)


def expander(heads, first, width):
    row = iota((2 * heads, width), 0)
    row = jnp.where(row >= heads, row - heads, row)
    return (row == (iota((2 * heads, width), 1) + first) // PH).astype(F32).astype(BF16)


def spread_heads(factors, first, width):
    high, low = split(factors.T)
    return dot(jnp.concatenate([high, low], axis=1), expander(factors.shape[0], first, width), 1, 0)


def states_kernel(where_ref, x_ref, g_ref, b_ref, c_ref, step_ref, log_ref, send_ref, own_ref):
    cum = running_sum(log_ref[...])
    from_source = step_ref[...] * jnp.exp(cum[:, TOK - 1 : TOK] - cum)
    from_start = jnp.exp(cum)

    def summed(values_ref, factors, map_ref, out_ref):
        doubled = jnp.concatenate([map_ref[...], map_ref[...]], axis=0)
        for first in range(0, HEADS * PH, QR):
            weighted = values_ref[:, first : first + QR].astype(F32) * spread_heads(factors, first, QR)
            high, low = split(weighted)
            out_ref[first : first + QR, :] = dot(jnp.concatenate([high, low], axis=0), doubled, 0, 0)

    forward = where_ref[0] == 1

    @pl.when(forward)
    def _():
        summed(g_ref, from_start, c_ref, send_ref)
        summed(x_ref, from_source, b_ref, own_ref)

    @pl.when(jnp.logical_not(forward))
    def _():
        summed(x_ref, from_source, b_ref, send_ref)
        summed(g_ref, from_start, c_ref, own_ref)


def chip_kernel(where_ref, decay_ref, got_ref, own_ref, *out_refs):
    place = where_ref[1]
    for k, out_ref in enumerate(out_refs):
        quarter = jnp.bitwise_xor(place, k)
        for j in range(QH):
            rows = pl.ds(pl.multiple_of(quarter * QR, QR) + j * PH, PH)
            out_ref[j * PH : (j + 1) * PH, :] = decay_ref[0, quarter * QH + j] * got_ref[rows, :] + own_ref[rows, :]


def group_kernel(where_ref, table_ref, *refs):
    parts, out_ref = refs[:4], refs[4]
    head = where_ref[1] * QH
    for j in range(QH):
        rows = slice(j * PH, (j + 1) * PH)
        total = table_ref[0, head + j] * parts[0][rows, :]
        for k in range(1, 4):
            total = total + table_ref[k, head + j] * parts[k][rows, :]
        out_ref[rows, :] = total


def prefix_kernel(where_ref, table_ref, *refs):
    parts, tops, out_refs = refs[:4], refs[4:7], refs[7:]
    head = where_ref[1] * QH
    for j in range(QH):
        rows = slice(j * PH, (j + 1) * PH)
        entering = table_ref[4, head + j] * tops[0][rows, :]
        for k in range(1, 3):
            entering = entering + table_ref[4 + k, head + j] * tops[k][rows, :]
        pieces = [p[rows, :] for p in parts]
        for k in range(4):
            total = table_ref[7 + k, head + j] * entering
            for i in range(4):
                if i != k:
                    total = total + table_ref[11 + 4 * k + i, head + j] * pieces[i]
            out_refs[k][rows, :] = total


def slab_kernel(x_ref, g_ref, b_ref, c_ref, step_ref, log_ref, after_ref, within_ref, back_ref, maps_ref, skip_ref, summed):
    quarter = pl.program_id(0)

    @pl.when(quarter == 0)
    def _():
        summed[...] = jnp.zeros_like(summed)

    affinity = dot(c_ref[...], b_ref[...], 1, 1)
    causal = iota((TOK, TOK), 0) >= iota((TOK, TOK), 1)
    cum = running_sum(log_ref[...])
    columns = cum.T
    left = iota((TOK, 2 * PH), 1) < PH
    zero = jnp.zeros((TOK, 2 * PH), BF16)
    for pair in range(QH // 2):
        lanes = slice(pair * 2 * PH, (pair + 1) * 2 * PH)
        x, g = x_ref[:, lanes], g_ref[:, lanes]
        xs = (jnp.where(left, x, zero), jnp.where(left, zero, x))
        gs = (jnp.where(left, g, zero), jnp.where(left, zero, g))
        mixes = []
        for side in range(2):
            j = 2 * pair + side
            gap = columns[:, j : j + 1] - cum[j : j + 1, :]
            decays = jnp.exp(jnp.where(causal, gap, -1e30)) * step_ref[j : j + 1, :]
            summed[...] += decays * dot(gs[side], x, 1, 1)
            mixes.extend(split(affinity * decays))
        within_ref[:, lanes] = dot(
            jnp.concatenate(mixes, axis=1), jnp.concatenate([xs[0], xs[0], xs[1], xs[1]], axis=0), 1, 0
        )
        back_ref[:, lanes] = dot(
            jnp.concatenate(mixes, axis=0), jnp.concatenate([gs[0], gs[0], gs[1], gs[1]], axis=0), 0, 0
        )
    products = jnp.sum(x_ref[...].astype(F32) * g_ref[...].astype(F32), axis=0, keepdims=True)
    owner = (iota((QH, QR), 1) // PH == iota((QH, QR), 0)).astype(F32)
    skip_ref[...] = jnp.broadcast_to(jnp.sum(owner * products, axis=1, keepdims=True), (QH, TOK))

    @pl.when(quarter == pl.num_programs(0) - 1)
    def _():
        high, low = split(summed[...])
        b, c = b_ref[...], c_ref[...]
        maps_ref[:, :NS] = dot(jnp.concatenate([high, low], axis=0), jnp.concatenate([c, c], axis=0), 0, 0)
        maps_ref[:, NS:] = dot(jnp.concatenate([high, low], axis=1), jnp.concatenate([b, b], axis=0), 1, 0)


def cross_kernel(
    where_ref, table_ref, x_ref, g_ref, within_ref, back_ref, step_ref, log_ref, gain_ref, b_ref, c_ref,
    near_ref, far_ref, first_ref, send_ref, own_ref, maps_in_ref, *refs,
):
    mixed_ref, ginputs_ref, gstep_ref, gdecay_ref, maps_ref, entering, arriving = refs[-7:]
    forward = where_ref[0] == 1
    head = where_ref[2] * QH
    cum = running_sum(log_ref[...])
    through = jnp.exp(cum[:, TOK - 1 : TOK])
    slots = []
    for j in range(QH):
        rows = slice(j * PH, (j + 1) * PH)
        slots.append(table_ref[27, head + j] * near_ref[rows, :] + first_ref[rows, :])
    scanned = jnp.concatenate(slots, axis=0)
    other = far_ref[...]
    entering[...] = jnp.where(forward, scanned, other)
    arriving[...] = jnp.where(forward, other, scanned)
    local = jnp.where(forward, own_ref[...], send_ref[...])

    x, g = x_ref[...].astype(F32), g_ref[...].astype(F32)
    starts = spread_heads(jnp.exp(cum), 0, QR)
    sources = spread_heads(step_ref[...] * jnp.exp(cum[:, TOK - 1 : TOK] - cum), 0, QR)
    ent, arr = entering[...], arriving[...]
    ent_high, ent_low = split(ent)
    arr_high, arr_low = split(arr)
    b, c = b_ref[...], c_ref[...]
    x_high, x_low = split(x * sources)
    maps_ref[:, :NS] = maps_in_ref[:, :NS] + (
        dot(x_high, arr_high, 1, 0) + (dot(x_low, arr_high, 1, 0) + dot(x_high, arr_low, 1, 0))
    )
    g_high, g_low = split(g * starts)
    maps_ref[:, NS:] = maps_in_ref[:, NS:] + (
        dot(g_high, ent_high, 1, 0) + (dot(g_low, ent_high, 1, 0) + dot(g_high, ent_low, 1, 0))
    )
    carried = dot(jnp.concatenate([c, c], axis=1), jnp.concatenate([ent_high, ent_low], axis=1), 1, 1) * starts
    later = dot(jnp.concatenate([b, b], axis=1), jnp.concatenate([arr_high, arr_low], axis=1), 1, 1) * sources
    output = within_ref[...] + carried
    back = back_ref[...] + later
    gain = gain_ref[...]
    mixed_ref[...] = (output + gain * x).astype(BF16)
    ginputs_ref[...] = (back + gain * g).astype(BF16)

    owner = (iota((QR, QH), 0) // PH == iota((QR, QH), 1)).astype(F32).astype(BF16)
    doubled = jnp.concatenate([owner, owner], axis=0)

    def by_head(values):
        high, low = split(values)
        return dot(jnp.concatenate([high, low], axis=1), doubled, 1, 0).T

    steps_part = x * back
    gstep_ref[...] = by_head(steps_part) / step_ref[...]
    change = by_head(g * output - steps_part)
    edges = []
    for j in range(QH):
        rows = slice(j * PH, (j + 1) * PH)
        leaving = local[rows, :] + through[j : j + 1, :] * ent[rows, :]
        edges.append(jnp.sum(arr[rows, :] * leaving, axis=0, keepdims=True))
    edge = jnp.sum(jnp.concatenate(edges, axis=0), axis=1, keepdims=True)
    change = change + jnp.where(iota((QH, TOK), 1) == TOK - 1, edge, 0.0)
    after = (iota((TOK, TOK), 0) >= iota((TOK, TOK), 1)).astype(F32)
    gdecay_ref[...] = dot(change, after, 1, 0, HIGHEST)


def call(kernel, outs, n_smem, n_in, scratch=()):
    smem = pl.BlockSpec(memory_space=pltpu.SMEM)
    vmem = pl.BlockSpec(memory_space=pltpu.VMEM)
    return pl.pallas_call(
        kernel,
        out_shape=[jax.ShapeDtypeStruct(s, F32) for s in outs],
        in_specs=[smem] * n_smem + [vmem] * n_in,
        out_specs=[vmem] * len(outs),
        scratch_shapes=list(scratch),
        compiler_params=pltpu.CompilerParams(vmem_limit_bytes=VMEM_LIMIT),
    )


def exchange(value, pairs):
    return lax.ppermute(value, "ctx", pairs)


def core_pairs(n):
    return [(i, i ^ 1) for i in range(n)]


def chip_pairs(n, k):
    return [(i, i ^ (2 * k)) for i in range(n)]


def group_pairs(n, k):
    pairs = [(i, i ^ (8 * k)) for i in range(n)]
    return [(i, j) for i, j in pairs if (j > i) == (i % 2 == 1)]


def decay_table(sums, me):
    forward = me % 2 == 1
    chip = me // 2
    base, place = (chip // 4) * 4, chip % 4
    group = chip // 4
    low, high, valid = [], [], []

    def add(f_low, f_high, f_ok, b_low, b_high, b_ok):
        low.append(jnp.where(forward, f_low, b_low))
        high.append(jnp.where(forward, f_high, b_high))
        valid.append(jnp.where(forward, f_ok, b_ok))

    for k in range(4):
        j = base + (place ^ k)
        add(j + 1, base + 4, True, base, j, True)
    for k in range(1, 4):
        s = group ^ k
        add(4 * (s + 1), 4 * group, s < group, 4 * (group + 1), 4 * s, s > group)
    for k in range(4):
        j = base + (place ^ k)
        add(base, j, True, j + 1, base + 4, True)
    for k in range(4):
        j = base + (place ^ k)
        for i in range(4):
            m = base + (place ^ i)
            add(m + 1, j, m < j, j + 1, m, m > j)
    low, high, valid = jnp.stack(low) * 2, jnp.stack(high) * 2, jnp.stack(valid)
    low = jnp.concatenate([low, (me ^ 1)[None]])
    high = jnp.concatenate([high, (me ^ 1)[None] + 1])
    valid = jnp.concatenate([valid, jnp.ones((1,), bool)])
    device = jnp.arange(sums.shape[0])
    inside = (device >= low[:, None]) & (device < high[:, None])
    total = jnp.sum(jnp.where(inside[:, :, None], sums[None], 0.0), axis=1)
    return jnp.where(valid[:, None], jnp.exp(total), 0.0)


def shards(inputs, grad_out, input_map, output_map, step_size, log_decay, skip_gain):
    n = lax.axis_size("ctx")
    me = lax.axis_index("ctx")
    x, g = inputs[0], grad_out[0]
    b, c = input_map[0], output_map[0]
    steps, logs = step_size[0], log_decay[0]
    features = HEADS * PH
    place = (me // 2) % 4
    where = [jnp.stack([me % 2, place, place ^ k]).astype(jnp.int32) for k in range(4)]

    sums = jnp.sum(logs, axis=1)
    table = decay_table(lax.all_gather(sums, "ctx"), me)

    send, own = call(states_kernel, [(features, NS)] * 2, 1, 6)(where[0], x, g, b, c, steps, logs)
    first = exchange(send, core_pairs(n))
    parts = call(chip_kernel, [(QR, NS)] * 4, 2, 2)(where[0], jnp.exp(sums)[None], first, own)
    mine = [parts[0]] + [exchange(parts[k], chip_pairs(n, k)) for k in range(1, 4)]

    quarter = lambda rows, cols, by_row: pl.BlockSpec((rows, cols), (lambda i: (i, 0)) if by_row else (lambda i: (0, i)))
    whole = lambda rows, cols: pl.BlockSpec((rows, cols), lambda i: (0, 0))
    within, back, maps, skips = pl.pallas_call(
        slab_kernel,
        grid=(HEADS // QH,),
        out_shape=[
            jax.ShapeDtypeStruct((TOK, features), F32),
            jax.ShapeDtypeStruct((TOK, features), F32),
            jax.ShapeDtypeStruct((TOK, 2 * NS), F32),
            jax.ShapeDtypeStruct((HEADS, TOK), F32),
        ],
        in_specs=[
            quarter(TOK, QR, False), quarter(TOK, QR, False), whole(TOK, NS), whole(TOK, NS),
            quarter(QH, TOK, True), quarter(QH, TOK, True), pl.BlockSpec((8, NS), lambda i: (0, 0)),
        ],
        out_specs=[quarter(TOK, QR, False), quarter(TOK, QR, False), whole(TOK, 2 * NS), quarter(QH, TOK, True)],
        scratch_shapes=[pltpu.VMEM((TOK, TOK), F32)],
        compiler_params=pltpu.CompilerParams(vmem_limit_bytes=VMEM_LIMIT),
    )(x, g, b, c, steps, logs, parts[0])
    skip_total = lax.psum(skips[:, 0], ("dp", "ctx"))

    (total,) = call(group_kernel, [(QR, NS)], 2, 4)(where[0], table, *mine)
    tops = [exchange(total, group_pairs(n, k)) for k in range(1, 4)]
    ready = call(prefix_kernel, [(QR, NS)] * 4, 2, 7)(where[0], table, *mine, *tops)
    near = [ready[0]] + [exchange(ready[k], chip_pairs(n, k)) for k in range(1, 4)]
    far = [exchange(near[k], core_pairs(n)) for k in range(4)]

    gains = jnp.repeat(skip_gain, PH)[None]
    outs = None
    shapes = [
        jax.ShapeDtypeStruct((TOK, features), BF16),
        jax.ShapeDtypeStruct((TOK, features), BF16),
        jax.ShapeDtypeStruct((HEADS, TOK), F32),
        jax.ShapeDtypeStruct((HEADS, TOK), F32),
        jax.ShapeDtypeStruct((TOK, 2 * NS), F32),
    ]
    for k in range(4):
        cols = pl.BlockSpec((TOK, QR), lambda i, w, t: (0, w[2]))
        rows = pl.BlockSpec((QH, TOK), lambda i, w, t: (w[2], 0))
        state = pl.BlockSpec((QR, NS), lambda i, w, t: (w[2], 0))
        fixed = lambda r, l: pl.BlockSpec((r, l), lambda i, w, t: (0, 0))
        in_specs = [
            cols, cols, cols, cols, rows, rows, pl.BlockSpec((1, QR), lambda i, w, t: (0, w[2])),
            fixed(TOK, NS), fixed(TOK, NS), fixed(QR, NS), fixed(QR, NS), state, state, state, fixed(TOK, 2 * NS),
        ]
        operands = [where[k], table, x, g, within, back, steps, logs, gains, b, c, near[k], far[k], first, send, own, maps]
        aliases = {}
        if k > 0:
            in_specs += [pl.BlockSpec(memory_space=pl.ANY)] * 4
            aliases = {len(operands) + i: i for i in range(4)}
            operands += outs[:4]
        outs = pl.pallas_call(
            cross_kernel,
            grid_spec=pltpu.PrefetchScalarGridSpec(
                num_scalar_prefetch=2,
                grid=(1,),
                in_specs=in_specs,
                out_specs=[cols, cols, rows, rows, fixed(TOK, 2 * NS)],
                scratch_shapes=[pltpu.VMEM((QR, NS), F32)] * 2,
            ),
            out_shape=shapes,
            input_output_aliases=aliases,
            compiler_params=pltpu.CompilerParams(vmem_limit_bytes=VMEM_LIMIT),
        )(*operands)
        maps = outs[4]
    mixed, ginputs, gstep, gdecay, maps = outs
    tp = lax.axis_size("tp")
    swapped = lax.all_to_all(maps.reshape(tp, TOK // tp, 2 * NS), "tp", 0, 0)
    reduced = jnp.sum(swapped, axis=0)
    factor = 1.0 / math.sqrt(lax.axis_size("dp") * TOK * n * PH)
    return (
        mixed[None],
        ginputs[None],
        gstep[None],
        gdecay[None],
        reduced[None, :, :NS],
        reduced[None, :, NS:],
        skip_total * factor,
    )


def solution(mesh):
    in_specs = (
        P("dp", "ctx", "tp"),
        P("dp", "ctx", "tp"),
        P("dp", "ctx", None),
        P("dp", "ctx", None),
        P("dp", "tp", "ctx"),
        P("dp", "tp", "ctx"),
        P("tp"),
    )
    out_specs = (
        P("dp", "ctx", "tp"),
        P("dp", "ctx", "tp"),
        P("dp", "tp", "ctx"),
        P("dp", "tp", "ctx"),
        P("dp", ("ctx", "tp"), None),
        P("dp", ("ctx", "tp"), None),
        P("tp"),
    )
    return jax.shard_map(shards, mesh=mesh, in_specs=in_specs, out_specs=out_specs, check_vma=False)
```

```python
import math

import jax
import jax.numpy as jnp
from jax import lax
from jax.experimental import pallas as pl
from jax.experimental.pallas import tpu as pltpu
from jax.sharding import PartitionSpec as P

F32 = jnp.float32
BF16 = jnp.bfloat16
HIGHEST = lax.Precision.HIGHEST
TOK = 128
HEADS = 32
PH = 64
NS = 128
FEATS = HEADS * PH
QH = 8
QR = QH * PH
CHUNKS = 2
CH = QH // CHUNKS
CR = CH * PH
SIDE = 2 * HEADS
VMEM_LIMIT = 48 * 1024 * 1024


def iota(shape, dim):
    return lax.broadcasted_iota(jnp.int32, shape, dim)


def split(value):
    high = value.astype(BF16)
    low = (value - high.astype(F32)).astype(BF16)
    return high, low


def dot(a, b, ca, cb, precision=None):
    return lax.dot_general(a, b, (((ca,), (cb,)), ((), ())), preferred_element_type=F32, precision=precision)


def running_sum(logs):
    upto = (iota((TOK, TOK), 0) <= iota((TOK, TOK), 1)).astype(F32)
    return dot(logs, upto, 1, 0, HIGHEST)


def expander(heads, first, width):
    row = iota((2 * heads, width), 0)
    row = jnp.where(row >= heads, row - heads, row)
    return (row == (iota((2 * heads, width), 1) + first) // PH).astype(F32).astype(BF16)


def spread_heads(factors, first, width):
    high, low = split(factors.T)
    return dot(jnp.concatenate([high, low], axis=1), expander(factors.shape[0], first, width), 1, 0)


def gate(flag, value):
    return jnp.where(flag, value, 0.0)


def states_kernel(own, where_ref, x_ref, g_ref, b_ref, c_ref, step_ref, log_ref, out_ref):
    cum = running_sum(log_ref[...])

    def summed(values_ref, factors, map_ref):
        doubled = jnp.concatenate([map_ref[...], map_ref[...]], axis=0)
        for first in range(0, FEATS, QR):
            weighted = values_ref[:, first : first + QR].astype(F32) * spread_heads(factors, first, QR)
            high, low = split(weighted)
            out_ref[first : first + QR, :] = dot(jnp.concatenate([high, low], axis=0), doubled, 0, 0)

    forward = where_ref[0] == (1 if own else 0)

    @pl.when(forward)
    def _():
        summed(x_ref, step_ref[...] * jnp.exp(cum[:, TOK - 1 : TOK] - cum), b_ref)

    @pl.when(jnp.logical_not(forward))
    def _():
        summed(g_ref, jnp.exp(cum), c_ref)

    out_ref[FEATS : FEATS + HEADS, :] = jnp.broadcast_to(cum[:, TOK - 1 : TOK], (HEADS, NS))
    products = jnp.sum(x_ref[...].astype(F32) * g_ref[...].astype(F32), axis=0, keepdims=True)
    owner = (iota((HEADS, FEATS), 1) // PH == iota((HEADS, FEATS), 0)).astype(F32)
    skips = jnp.sum(owner * products, axis=1, keepdims=True)
    out_ref[FEATS + HEADS : FEATS + SIDE, :] = jnp.broadcast_to(skips, (HEADS, NS))


def chip_kernel(where_ref, got_ref, own_ref, *out_refs):
    place = where_ref[1]
    for k in range(4):
        quarter = jnp.bitwise_xor(place, k)
        rows = pl.ds(pl.multiple_of(FEATS + quarter * QH, QH), QH)
        logs, got_logs = own_ref[rows, :], got_ref[rows, :]
        rows = pl.ds(pl.multiple_of(FEATS + HEADS + quarter * QH, QH), QH)
        skips = own_ref[rows, :] + got_ref[rows, :]
        decay = jnp.exp(logs)
        logs = logs + got_logs
        for part in range(CHUNKS):
            out_ref = out_refs[k * CHUNKS + part]
            for j in range(CH):
                h = part * CH + j
                rows = pl.ds(pl.multiple_of(quarter * QR + h * PH, PH), PH)
                out_ref[j * PH : (j + 1) * PH, :] = decay[h : h + 1, :] * got_ref[rows, :] + own_ref[rows, :]
            heads = slice(part * CH, (part + 1) * CH)
            out_ref[CR : CR + CH, :] = logs[heads, :]
            out_ref[CR + CH : CR + 2 * CH, :] = skips[heads, :]


def order(where_ref, index):
    me = where_ref[index]
    places = [jnp.bitwise_xor(me, k) for k in range(4)]
    return [jnp.where(where_ref[0] == 1, p, 3 - p) for p in places]


def group_kernel(where_ref, *refs):
    parts, out_ref = refs[:4], refs[4]
    place = order(where_ref, 1)
    logs = [p[CR : CR + CH, :] for p in parts]
    weights = []
    for k in range(4):
        later = [gate(place[i] > place[k], logs[i]) for i in range(4) if i != k]
        weights.append(jnp.exp(later[0] + later[1] + later[2]))
    for j in range(CH):
        rows = slice(j * PH, (j + 1) * PH)
        terms = [weights[k][j : j + 1, :] * parts[k][rows, :] for k in range(4)]
        out_ref[rows, :] = (terms[0] + terms[1]) + (terms[2] + terms[3])
    side = slice(CR, CR + 2 * CH)
    out_ref[side, :] = (parts[0][side, :] + parts[1][side, :]) + (parts[2][side, :] + parts[3][side, :])


def prefix_kernel(where_ref, *refs):
    place, group = order(where_ref, 1), order(where_ref, 3)
    out_refs = refs[7 * CHUNKS :]
    skips = []
    for part in range(CHUNKS):
        parts, tops = refs[7 * part : 7 * part + 4], refs[7 * part + 4 : 7 * part + 7]
        logs = [p[CR : CR + CH, :] for p in parts]
        top_logs = [t[CR : CR + CH, :] for t in tops]
        top_weights = []
        for k in range(3):
            between = [
                gate((group[k + 1] < group[i + 1]) & (group[i + 1] < group[0]), top_logs[i])
                for i in range(3)
                if i != k
            ]
            top_weights.append(jnp.exp(between[0] + between[1]))
        group_weights, pair_weights = [], {}
        for k in range(4):
            before = [gate(place[i] < place[k], logs[i]) for i in range(4) if i != k]
            group_weights.append(jnp.exp(before[0] + before[1] + before[2]))
            for i in range(4):
                if i != k:
                    between = [
                        gate((place[i] < place[m]) & (place[m] < place[k]), logs[m])
                        for m in range(4)
                        if m not in (i, k)
                    ]
                    pair_weights[k, i] = gate(place[i] < place[k], jnp.exp(between[0] + between[1]))
        for j in range(CH):
            rows = slice(j * PH, (j + 1) * PH)
            at = slice(j, j + 1)
            entering = top_weights[0][at, :] * tops[0][rows, :] + top_weights[1][at, :] * tops[1][rows, :]
            entering = entering + top_weights[2][at, :] * tops[2][rows, :]
            pieces = [p[rows, :] for p in parts]
            first = (part * CH + j) * PH
            for k in range(4):
                total = group_weights[k][at, :] * entering
                for i in range(4):
                    if i != k:
                        total = total + pair_weights[k, i][at, :] * pieces[i]
                out_refs[k][first : first + PH, :] = total
        side = slice(CR + CH, CR + 2 * CH)
        mine = (parts[0][side, :] + parts[1][side, :]) + (parts[2][side, :] + parts[3][side, :])
        skips.append(gate(where_ref[0] == 1, mine) + (tops[0][side, :] + tops[1][side, :] + tops[2][side, :]))
    for k in range(4):
        out_refs[k][QR : QR + QH, :] = jnp.concatenate(skips, axis=0)


def slab_kernel(x_ref, g_ref, b_ref, c_ref, step_ref, log_ref, after_ref, within_ref, back_ref, maps_ref, summed):
    quarter = pl.program_id(0)

    @pl.when(quarter == 0)
    def _():
        summed[...] = jnp.zeros_like(summed)

    affinity = dot(c_ref[...], b_ref[...], 1, 1)
    causal = iota((TOK, TOK), 0) >= iota((TOK, TOK), 1)
    cum = running_sum(log_ref[...])
    columns = cum.T
    left = iota((TOK, 2 * PH), 1) < PH
    zero = jnp.zeros((TOK, 2 * PH), BF16)
    for pair in range(QH // 2):
        lanes = slice(pair * 2 * PH, (pair + 1) * 2 * PH)
        x, g = x_ref[:, lanes], g_ref[:, lanes]
        xs = (jnp.where(left, x, zero), jnp.where(left, zero, x))
        gs = (jnp.where(left, g, zero), jnp.where(left, zero, g))
        mixes = []
        for side in range(2):
            j = 2 * pair + side
            gap = columns[:, j : j + 1] - cum[j : j + 1, :]
            decays = jnp.exp(jnp.where(causal, gap, -1e30)) * step_ref[j : j + 1, :]
            summed[...] += decays * dot(gs[side], x, 1, 1)
            mixes.extend(split(affinity * decays))
        within_ref[:, lanes] = dot(
            jnp.concatenate(mixes, axis=1), jnp.concatenate([xs[0], xs[0], xs[1], xs[1]], axis=0), 1, 0
        )
        back_ref[:, lanes] = dot(
            jnp.concatenate(mixes, axis=0), jnp.concatenate([gs[0], gs[0], gs[1], gs[1]], axis=0), 0, 0
        )

    @pl.when(quarter == pl.num_programs(0) - 1)
    def _():
        high, low = split(summed[...])
        b, c = b_ref[...], c_ref[...]
        maps_ref[:, :NS] = dot(jnp.concatenate([high, low], axis=0), jnp.concatenate([c, c], axis=0), 0, 0)
        maps_ref[:, NS:] = dot(jnp.concatenate([high, low], axis=1), jnp.concatenate([b, b], axis=0), 1, 0)


def cross_kernel(
    last, where_ref, x_ref, g_ref, within_ref, back_ref, step_ref, log_ref, gain_ref, b_ref, c_ref,
    near_ref, far_ref, first_ref, other_ref, send_ref, own_ref, maps_in_ref, *refs,
):
    count = 9 if last else 6
    mixed_ref, ginputs_ref, gstep_ref, gdecay_ref, skip_ref = refs[-count : 5 - count]
    maps_refs = refs[5 - count :]
    forward = where_ref[0] == 1
    cum = running_sum(log_ref[...])
    through = jnp.exp(cum[:, TOK - 1 : TOK])
    skip_ref[...] = near_ref[QR : QR + QH, :] + far_ref[QR : QR + QH, :]
    decay = jnp.exp(other_ref[...])
    slots = []
    for j in range(QH):
        rows = slice(j * PH, (j + 1) * PH)
        slots.append(decay[j : j + 1, :] * near_ref[rows, :] + first_ref[rows, :])
    scanned = jnp.concatenate(slots, axis=0)
    other = far_ref[:QR, :]
    ent = jnp.where(forward, scanned, other)
    arr = jnp.where(forward, other, scanned)

    x, g = x_ref[...].astype(F32), g_ref[...].astype(F32)
    starts = spread_heads(jnp.exp(cum), 0, QR)
    sources = spread_heads(step_ref[...] * jnp.exp(cum[:, TOK - 1 : TOK] - cum), 0, QR)
    ent_high, ent_low = split(ent)
    arr_high, arr_low = split(arr)
    b, c = b_ref[...], c_ref[...]
    x_high, x_low = split(x * sources)
    from_arr = dot(x_high, arr_high, 1, 0) + (dot(x_low, arr_high, 1, 0) + dot(x_high, arr_low, 1, 0))
    g_high, g_low = split(g * starts)
    from_ent = dot(g_high, ent_high, 1, 0) + (dot(g_low, ent_high, 1, 0) + dot(g_high, ent_low, 1, 0))
    maps = maps_in_ref[...] + jnp.concatenate([from_arr, from_ent], axis=1)
    if last:
        rows = TOK // 4
        for k in range(4):
            part = jnp.bitwise_xor(where_ref[4], k)
            total = gate(part == 0, maps[:rows, :])
            for i in range(1, 4):
                total = jnp.where(part == i, maps[i * rows : (i + 1) * rows, :], total)
            maps_refs[k][...] = total
    else:
        maps_refs[0][...] = maps
    carried = dot(jnp.concatenate([c, c], axis=1), jnp.concatenate([ent_high, ent_low], axis=1), 1, 1) * starts
    later = dot(jnp.concatenate([b, b], axis=1), jnp.concatenate([arr_high, arr_low], axis=1), 1, 1) * sources
    output = within_ref[...] + carried
    back = back_ref[...] + later
    gain = gain_ref[...]
    mixed_ref[...] = (output + gain * x).astype(BF16)
    ginputs_ref[...] = (back + gain * g).astype(BF16)

    owner = (iota((QR, QH), 0) // PH == iota((QR, QH), 1)).astype(F32).astype(BF16)
    doubled = jnp.concatenate([owner, owner], axis=0)

    def by_head(values):
        high, low = split(values)
        return dot(jnp.concatenate([high, low], axis=1), doubled, 1, 0).T

    steps_part = x * back
    gstep_ref[...] = by_head(steps_part) / step_ref[...]
    change = by_head(g * output - steps_part)
    local = jnp.where(forward, own_ref[...], send_ref[...])
    edges = []
    for j in range(QH):
        rows = slice(j * PH, (j + 1) * PH)
        leaving = local[rows, :] + through[j : j + 1, :] * ent[rows, :]
        edges.append(jnp.sum(arr[rows, :] * leaving, axis=0, keepdims=True))
    edge = jnp.sum(jnp.concatenate(edges, axis=0), axis=1, keepdims=True)
    change = change + jnp.where(iota((QH, TOK), 1) == TOK - 1, edge, 0.0)
    after = (iota((TOK, TOK), 0) >= iota((TOK, TOK), 1)).astype(F32)
    gdecay_ref[...] = dot(change, after, 1, 0, HIGHEST)


def call(kernel, outs, n_in):
    smem = pl.BlockSpec(memory_space=pltpu.SMEM)
    vmem = pl.BlockSpec(memory_space=pltpu.VMEM)
    return pl.pallas_call(
        kernel,
        out_shape=[jax.ShapeDtypeStruct(s, F32) for s in outs],
        in_specs=[smem] + [vmem] * n_in,
        out_specs=[vmem] * len(outs),
        compiler_params=pltpu.CompilerParams(vmem_limit_bytes=VMEM_LIMIT),
    )


def tied(value, *others):
    return lax.optimization_barrier((value, *others))[0]


def core_pairs(n):
    return [(i, i ^ 1) for i in range(n)]


def chip_pairs(n, k):
    return [(i, i ^ (2 * k)) for i in range(n)]


def group_pairs(n, k):
    pairs = [(i, i ^ (8 * k)) for i in range(n)]
    return [(i, j) for i, j in pairs if (j > i) == (i % 2 == 1)]


def partners(value, axis, k):
    n = lax.axis_size(axis)
    return lax.ppermute(value, axis, [(i, i ^ k) for i in range(n) if i ^ k < n])


def shards(inputs, grad_out, input_map, output_map, step_size, log_decay, skip_gain):
    n = lax.axis_size("ctx")
    me = lax.axis_index("ctx")
    x, g = inputs[0], grad_out[0]
    b, c = input_map[0], output_map[0]
    steps, logs = step_size[0], log_decay[0]
    place, group = (me // 2) % 4, me // 8
    member = lax.axis_index("tp")
    where = [jnp.stack([me % 2, place, place ^ k, group, member]).astype(jnp.int32) for k in range(4)]
    gains = jnp.repeat(skip_gain, PH)[None]
    slab = [(FEATS + SIDE, NS)]

    def states(own):
        return call(lambda *refs: states_kernel(own, *refs), slab, 6)(where[0], x, g, b, c, steps, logs)[0]

    send = states(False)
    first = lax.ppermute(send, "ctx", core_pairs(n))
    own = states(True)
    piece = (CR + 2 * CH, NS)
    parts = call(chip_kernel, [piece] * (4 * CHUNKS), 2)(where[0], first, own)
    mine = []
    for i in range(CHUNKS):
        mine.append([parts[i]] + [lax.ppermute(parts[k * CHUNKS + i], "ctx", chip_pairs(n, k)) for k in range(1, 4)])

    quarter = lambda rows, cols, by_row: pl.BlockSpec((rows, cols), (lambda i: (i, 0)) if by_row else (lambda i: (0, i)))
    whole = lambda rows, cols: pl.BlockSpec((rows, cols), lambda i: (0, 0))
    within, back, maps = pl.pallas_call(
        slab_kernel,
        grid=(HEADS // QH,),
        out_shape=[
            jax.ShapeDtypeStruct((TOK, FEATS), F32),
            jax.ShapeDtypeStruct((TOK, FEATS), F32),
            jax.ShapeDtypeStruct((TOK, 2 * NS), F32),
        ],
        in_specs=[
            quarter(TOK, QR, False), quarter(TOK, QR, False), whole(TOK, NS), whole(TOK, NS),
            quarter(QH, TOK, True), quarter(QH, TOK, True), whole(8, NS),
        ],
        out_specs=[quarter(TOK, QR, False), quarter(TOK, QR, False), whole(TOK, 2 * NS)],
        scratch_shapes=[pltpu.VMEM((TOK, TOK), F32)],
        compiler_params=pltpu.CompilerParams(vmem_limit_bytes=VMEM_LIMIT),
    )(x, g, b, c, steps, logs, mine[0][1])

    gathered = []
    for i in range(CHUNKS):
        (total,) = call(group_kernel, [piece], 4)(where[0], *mine[i])
        gathered.append(mine[i] + [lax.ppermute(total, "ctx", group_pairs(n, k)) for k in range(1, 4)])
    ready = call(prefix_kernel, [(QR + QH, NS)] * 4, 7 * CHUNKS)(where[0], *sum(gathered, []))
    near = [ready[0]] + [lax.ppermute(ready[k], "ctx", chip_pairs(n, k)) for k in range(1, 4)]

    outs = None
    shapes = [
        jax.ShapeDtypeStruct((TOK, FEATS), BF16),
        jax.ShapeDtypeStruct((TOK, FEATS), BF16),
        jax.ShapeDtypeStruct((HEADS, TOK), F32),
        jax.ShapeDtypeStruct((HEADS, TOK), F32),
        jax.ShapeDtypeStruct((HEADS, TOK), F32),
    ]
    for k in range(4):
        last = k == 3
        passed = near[k] if k == 0 else tied(near[k], maps)
        far = lax.ppermute(passed, "ctx", core_pairs(n))
        cols = pl.BlockSpec((TOK, QR), lambda i, w: (0, w[2]))
        rows = pl.BlockSpec((QH, TOK), lambda i, w: (w[2], 0))
        state = pl.BlockSpec((QR, NS), lambda i, w: (w[2], 0))
        others = pl.BlockSpec((QH, NS), lambda i, w: (FEATS // QH + w[2], 0))
        fixed = lambda r, l: pl.BlockSpec((r, l), lambda i, w: (0, 0))
        in_specs = [
            cols, cols, cols, cols, rows, rows, pl.BlockSpec((1, QR), lambda i, w: (0, w[2])),
            fixed(TOK, NS), fixed(TOK, NS), fixed(QR + QH, NS), fixed(QR + QH, NS), state, others, state, state,
            fixed(TOK, 2 * NS),
        ]
        operands = [where[k], x, g, within, back, steps, logs, gains, b, c, passed, far, first, first, send, own, maps]
        aliases = {}
        if k > 0:
            in_specs += [pl.BlockSpec(memory_space=pl.ANY)] * 5
            aliases = {len(operands) + i: i for i in range(5)}
            operands += outs[:5]
        ends = [(TOK // 4, 2 * NS)] * 4 if last else [(TOK, 2 * NS)]
        outs = pl.pallas_call(
            lambda *refs, last=last: cross_kernel(last, *refs),
            grid_spec=pltpu.PrefetchScalarGridSpec(
                num_scalar_prefetch=1,
                grid=(1,),
                in_specs=in_specs,
                out_specs=[cols, cols, rows, rows, rows] + [fixed(*e) for e in ends],
            ),
            out_shape=shapes + [jax.ShapeDtypeStruct(e, F32) for e in ends],
            input_output_aliases=aliases,
            compiler_params=pltpu.CompilerParams(vmem_limit_bytes=VMEM_LIMIT),
        )(*operands)
        maps = outs[5]
    mixed, ginputs, gstep, gdecay, skips = outs[:5]
    reduced = outs[5]
    for k in range(1, 4):
        reduced = reduced + partners(outs[5 + k], "tp", k)
    skip = skips[:, 0]
    skip_total = skip + partners(skip, "dp", 1) + partners(skip, "dp", 2) + partners(skip, "dp", 3)
    factor = 1.0 / math.sqrt(lax.axis_size("dp") * TOK * n * PH)
    return (
        mixed[None],
        ginputs[None],
        gstep[None],
        gdecay[None],
        reduced[None, :, :NS],
        reduced[None, :, NS:],
        skip_total * factor,
    )


def solution(mesh):
    in_specs = (
        P("dp", "ctx", "tp"),
        P("dp", "ctx", "tp"),
        P("dp", "ctx", None),
        P("dp", "ctx", None),
        P("dp", "tp", "ctx"),
        P("dp", "tp", "ctx"),
        P("tp"),
    )
    out_specs = (
        P("dp", "ctx", "tp"),
        P("dp", "ctx", "tp"),
        P("dp", "tp", "ctx"),
        P("dp", "tp", "ctx"),
        P("dp", ("ctx", "tp"), None),
        P("dp", ("ctx", "tp"), None),
        P("tp"),
    )
    return jax.shard_map(shards, mesh=mesh, in_specs=in_specs, out_specs=out_specs, check_vma=False)
```

```python
import math

import jax
import jax.numpy as jnp
from jax import lax
from jax.experimental import pallas as pl
from jax.experimental.pallas import tpu as pltpu
from jax.sharding import PartitionSpec as P

F32 = jnp.float32
BF16 = jnp.bfloat16
HIGHEST = lax.Precision.HIGHEST
TOK = 128
HEADS = 32
PH = 64
NS = 128
FEATS = HEADS * PH
QH = 8
QR = QH * PH
PIECE = QR + 2 * QH
NEAR = QR + QH
SIDE = 2 * HEADS
VMEM_LIMIT = 48 * 1024 * 1024


def iota(shape, dim):
    return lax.broadcasted_iota(jnp.int32, shape, dim)


def split(value):
    high = value.astype(BF16)
    low = (value - high.astype(F32)).astype(BF16)
    return high, low


def dot(a, b, ca, cb, precision=None):
    return lax.dot_general(a, b, (((ca,), (cb,)), ((), ())), preferred_element_type=F32, precision=precision)


def running_sum(logs):
    upto = (iota((TOK, TOK), 0) <= iota((TOK, TOK), 1)).astype(F32)
    return dot(logs, upto, 1, 0, HIGHEST)


def expander(heads, first, width):
    row = iota((2 * heads, width), 0)
    row = jnp.where(row >= heads, row - heads, row)
    return (row == (iota((2 * heads, width), 1) + first) // PH).astype(F32).astype(BF16)


def spread_heads(factors, first, width):
    high, low = split(factors.T)
    return dot(jnp.concatenate([high, low], axis=1), expander(factors.shape[0], first, width), 1, 0)


def gate(flag, value):
    return jnp.where(flag, value, 0.0)


def states_kernel(own, where_ref, x_ref, g_ref, b_ref, c_ref, step_ref, log_ref, out_ref, *scratch):
    if scratch:
        held, sems = scratch[:6], scratch[6]
        copies = [
            pltpu.make_async_copy(ref, slot, sems.at[i])
            for i, (ref, slot) in enumerate(zip((x_ref, g_ref, b_ref, c_ref, step_ref, log_ref), held, strict=True))
        ]
        for copy in copies:
            copy.start()
        for copy in copies:
            copy.wait()
        x_ref, g_ref, b_ref, c_ref, step_ref, log_ref = held
    cum = running_sum(log_ref[...])

    def summed(values_ref, factors, map_ref):
        doubled = jnp.concatenate([map_ref[...], map_ref[...]], axis=0)
        for first in range(0, FEATS, QR):
            weighted = values_ref[:, first : first + QR].astype(F32) * spread_heads(factors, first, QR)
            high, low = split(weighted)
            out_ref[first : first + QR, :] = dot(jnp.concatenate([high, low], axis=0), doubled, 0, 0)

    forward = where_ref[0] == (1 if own else 0)

    @pl.when(forward)
    def _():
        summed(x_ref, step_ref[...] * jnp.exp(cum[:, TOK - 1 : TOK] - cum), b_ref)

    @pl.when(jnp.logical_not(forward))
    def _():
        summed(g_ref, jnp.exp(cum), c_ref)

    out_ref[FEATS : FEATS + HEADS, :] = jnp.broadcast_to(cum[:, TOK - 1 : TOK], (HEADS, NS))
    products = jnp.sum(x_ref[...].astype(F32) * g_ref[...].astype(F32), axis=0, keepdims=True)
    owner = (iota((HEADS, FEATS), 1) // PH == iota((HEADS, FEATS), 0)).astype(F32)
    skips = jnp.sum(owner * products, axis=1, keepdims=True)
    out_ref[FEATS + HEADS : FEATS + SIDE, :] = jnp.broadcast_to(skips, (HEADS, NS))


def chip_kernel(where_ref, got_ref, own_ref, *out_refs):
    place = where_ref[2]
    for k, out_ref in enumerate(out_refs):
        quarter = jnp.bitwise_xor(place, k)
        rows = pl.ds(pl.multiple_of(FEATS + quarter * QH, QH), QH)
        logs, got_logs = own_ref[rows, :], got_ref[rows, :]
        decay = jnp.exp(logs)
        for j in range(QH):
            rows = pl.ds(pl.multiple_of(quarter * QR + j * PH, PH), PH)
            out_ref[j * PH : (j + 1) * PH, :] = decay[j : j + 1, :] * got_ref[rows, :] + own_ref[rows, :]
        out_ref[QR : QR + QH, :] = logs + got_logs
        rows = pl.ds(pl.multiple_of(FEATS + HEADS + quarter * QH, QH), QH)
        out_ref[QR + QH : PIECE, :] = own_ref[rows, :] + got_ref[rows, :]


def group_kernel(where_ref, *refs):
    got, out_ref, parts_ref = refs[:4], refs[4], refs[5]
    forward = where_ref[0] == 1
    place = where_ref[2]
    for k in range(4):
        parts_ref[pl.ds(pl.multiple_of(jnp.bitwise_xor(place, k) * PIECE, 8), PIECE), :] = got[k][...]
    logs = [parts_ref[k * PIECE + QR : k * PIECE + QR + QH, :] for k in range(4)]
    none = jnp.zeros_like(logs[0])
    weights = [jnp.exp(jnp.where(forward, sum(logs[k + 1 :], none), sum(logs[:k], none))) for k in range(4)]
    for j in range(QH):
        terms = [
            weights[k][j : j + 1, :] * parts_ref[k * PIECE + j * PH : k * PIECE + (j + 1) * PH, :] for k in range(4)
        ]
        out_ref[j * PH : (j + 1) * PH, :] = (terms[0] + terms[1]) + (terms[2] + terms[3])
    side = [parts_ref[k * PIECE + QR : (k + 1) * PIECE, :] for k in range(4)]
    out_ref[QR:PIECE, :] = (side[0] + side[1]) + (side[2] + side[3])


def prefix_kernel(where_ref, parts_ref, *refs):
    forward = where_ref[0] == 1
    me = where_ref[1]
    group = [jnp.bitwise_xor(me, k) for k in range(4)]
    group = [jnp.where(forward, p, 3 - p) for p in group]
    tops, out_ref = refs[:3], refs[3]
    top_logs = [t[QR : QR + QH, :] for t in tops]
    weights = []
    for k in range(3):
        between = [
            gate((group[k + 1] < group[i + 1]) & (group[i + 1] < group[0]), top_logs[i]) for i in range(3) if i != k
        ]
        weights.append(jnp.exp(between[0] + between[1]))
    decays = [jnp.exp(parts_ref[k * PIECE + QR : k * PIECE + QR + QH, :]) for k in range(4)]

    def scan(sequence, carries_own):
        for j in range(QH):
            rows = slice(j * PH, (j + 1) * PH)
            at = slice(j, j + 1)
            state = weights[0][at, :] * tops[0][rows, :] + weights[1][at, :] * tops[1][rows, :]
            state = state + weights[2][at, :] * tops[2][rows, :]
            for k in sequence:
                out_ref[k * NEAR + j * PH : k * NEAR + (j + 1) * PH, :] = state
                if k != sequence[-1]:
                    state = decays[k][at, :] * state + parts_ref[k * PIECE + j * PH : k * PIECE + (j + 1) * PH, :]
        skips = tops[0][QR + QH :, :] + tops[1][QR + QH :, :] + tops[2][QR + QH :, :]
        if carries_own:
            for k in range(4):
                skips = skips + parts_ref[k * PIECE + QR + QH : (k + 1) * PIECE, :]
        for k in range(4):
            out_ref[k * NEAR + QR : (k + 1) * NEAR, :] = skips

    @pl.when(forward)
    def _():
        scan((0, 1, 2, 3), True)

    @pl.when(jnp.logical_not(forward))
    def _():
        scan((3, 2, 1, 0), False)


def slab_kernel(x_ref, g_ref, b_ref, c_ref, step_ref, log_ref, after_ref, within_ref, back_ref, maps_ref, summed):
    quarter = pl.program_id(0)

    @pl.when(quarter == 0)
    def _():
        summed[...] = jnp.zeros_like(summed)

    affinity = dot(c_ref[...], b_ref[...], 1, 1)
    causal = iota((TOK, TOK), 0) >= iota((TOK, TOK), 1)
    cum = running_sum(log_ref[...])
    columns = cum.T
    left = iota((TOK, 2 * PH), 1) < PH
    zero = jnp.zeros((TOK, 2 * PH), BF16)
    for pair in range(QH // 2):
        lanes = slice(pair * 2 * PH, (pair + 1) * 2 * PH)
        x, g = x_ref[:, lanes], g_ref[:, lanes]
        xs = (jnp.where(left, x, zero), jnp.where(left, zero, x))
        gs = (jnp.where(left, g, zero), jnp.where(left, zero, g))
        mixes = []
        for side in range(2):
            j = 2 * pair + side
            gap = columns[:, j : j + 1] - cum[j : j + 1, :]
            decays = jnp.exp(jnp.where(causal, gap, -1e30)) * step_ref[j : j + 1, :]
            summed[...] += decays * dot(gs[side], x, 1, 1)
            mixes.extend(split(affinity * decays))
        within_ref[:, lanes] = dot(
            jnp.concatenate(mixes, axis=1), jnp.concatenate([xs[0], xs[0], xs[1], xs[1]], axis=0), 1, 0
        )
        back_ref[:, lanes] = dot(
            jnp.concatenate(mixes, axis=0), jnp.concatenate([gs[0], gs[0], gs[1], gs[1]], axis=0), 0, 0
        )

    @pl.when(quarter == pl.num_programs(0) - 1)
    def _():
        high, low = split(summed[...])
        b, c = b_ref[...], c_ref[...]
        maps_ref[:, :NS] = dot(jnp.concatenate([high, low], axis=0), jnp.concatenate([c, c], axis=0), 0, 0)
        maps_ref[:, NS:] = dot(jnp.concatenate([high, low], axis=1), jnp.concatenate([b, b], axis=0), 1, 0)


def at_slab(quarter, near_ref, first_ref):
    decay = jnp.exp(first_ref[FEATS + quarter * QH : FEATS + (quarter + 1) * QH, :])
    slots = []
    for j in range(QH):
        near = near_ref[quarter * NEAR + j * PH : quarter * NEAR + (j + 1) * PH, :]
        first = quarter * QR + j * PH
        slots.append(decay[j : j + 1, :] * near + first_ref[first : first + PH, :])
    return jnp.concatenate(slots, axis=0)


def weighted_sum(forward, x_ref, g_ref, step_ref, log_ref, state_of):
    cum = running_sum(log_ref[...])
    factors = jnp.where(forward, jnp.exp(cum), step_ref[...] * jnp.exp(cum[:, TOK - 1 : TOK] - cum))
    total = jnp.zeros((TOK, NS), F32)
    for quarter in range(4):
        lanes = slice(quarter * QR, (quarter + 1) * QR)
        values = jnp.where(forward, g_ref[:, lanes].astype(F32), x_ref[:, lanes].astype(F32))
        high, low = split(values * spread_heads(factors, quarter * QR, QR))
        state_high, state_low = split(state_of(quarter))
        total = total + (dot(high, state_high, 1, 0) + (dot(low, state_high, 1, 0) + dot(high, state_low, 1, 0)))
    return total


def near_maps_kernel(where_ref, x_ref, g_ref, step_ref, log_ref, near_ref, first_ref, out_ref):
    out_ref[...] = weighted_sum(
        where_ref[0] == 1, x_ref, g_ref, step_ref, log_ref, lambda quarter: at_slab(quarter, near_ref, first_ref)
    )


def far_maps_kernel(
    where_ref, x_ref, g_ref, step_ref, log_ref, near_ref, far_ref, maps_in_ref, near_maps_ref, maps_ref, skip_ref
):
    forward = where_ref[0] == 1
    other = weighted_sum(
        where_ref[0] == 0, x_ref, g_ref, step_ref, log_ref,
        lambda quarter: far_ref[quarter * NEAR : quarter * NEAR + QR, :],
    )
    for quarter in range(4):
        side = slice(quarter * NEAR + QR, (quarter + 1) * NEAR)
        skip_ref[quarter * QH : (quarter + 1) * QH, :] = near_ref[side, :] + far_ref[side, :]
    mine = near_maps_ref[...]
    maps_ref[:, :NS] = maps_in_ref[:, :NS] + jnp.where(forward, other, mine)
    maps_ref[:, NS:] = maps_in_ref[:, NS:] + jnp.where(forward, mine, other)


def cross_kernel(
    where_ref, x_ref, g_ref, within_ref, back_ref, step_ref, log_ref, gain_ref, b_ref, c_ref,
    near_ref, far_ref, first_ref, send_ref, own_ref,
    mixed_ref, ginputs_ref, gstep_ref, gdecay_ref,
):
    forward = where_ref[0] == 1
    cums = running_sum(log_ref[...])
    b, c = b_ref[...], c_ref[...]
    two_b, two_c = jnp.concatenate([b, b], axis=1), jnp.concatenate([c, c], axis=1)
    owner = (iota((QR, QH), 0) // PH == iota((QR, QH), 1)).astype(F32).astype(BF16)
    doubled = jnp.concatenate([owner, owner], axis=0)
    after = (iota((TOK, TOK), 0) >= iota((TOK, TOK), 1)).astype(F32)

    def by_head(values):
        return dot(jnp.concatenate(split(values), axis=1), doubled, 1, 0).T

    for quarter in range(4):
        lanes = slice(quarter * QR, (quarter + 1) * QR)
        heads = slice(quarter * QH, (quarter + 1) * QH)
        cum, steps = cums[heads, :], step_ref[heads, :]
        through = jnp.exp(cum[:, TOK - 1 : TOK])
        scanned = at_slab(quarter, near_ref, first_ref)
        other = far_ref[quarter * NEAR : quarter * NEAR + QR, :]
        ent = jnp.where(forward, scanned, other)
        arr = jnp.where(forward, other, scanned)
        x, g = x_ref[:, lanes].astype(F32), g_ref[:, lanes].astype(F32)
        starts = spread_heads(jnp.exp(cum), 0, QR)
        sources = spread_heads(steps * jnp.exp(cum[:, TOK - 1 : TOK] - cum), 0, QR)
        output = within_ref[:, lanes] + dot(two_c, jnp.concatenate(split(ent), axis=1), 1, 1) * starts
        back = back_ref[:, lanes] + dot(two_b, jnp.concatenate(split(arr), axis=1), 1, 1) * sources
        gain = gain_ref[:, lanes]
        mixed_ref[:, lanes] = (output + gain * x).astype(BF16)
        ginputs_ref[:, lanes] = (back + gain * g).astype(BF16)
        steps_part = x * back
        gstep_ref[heads, :] = by_head(steps_part) / steps
        change = by_head(g * output - steps_part)
        edges = []
        for j in range(QH):
            rows = slice(quarter * QR + j * PH, quarter * QR + (j + 1) * PH)
            local = jnp.where(forward, own_ref[rows, :], send_ref[rows, :])
            rows = slice(j * PH, (j + 1) * PH)
            leaving = local + through[j : j + 1, :] * ent[rows, :]
            edges.append(jnp.sum(arr[rows, :] * leaving, axis=0, keepdims=True))
        edge = jnp.sum(jnp.concatenate(edges, axis=0), axis=1, keepdims=True)
        change = change + jnp.where(iota((QH, TOK), 1) == TOK - 1, edge, 0.0)
        gdecay_ref[heads, :] = dot(change, after, 1, 0, HIGHEST)


PARAMS = pltpu.CompilerParams(vmem_limit_bytes=VMEM_LIMIT)


def call(kernel, outs, n_in, space=pltpu.VMEM, scratch=()):
    smem = pl.BlockSpec(memory_space=pltpu.SMEM)
    vmem = pl.BlockSpec(memory_space=pltpu.VMEM)
    return pl.pallas_call(
        kernel,
        out_shape=[jax.ShapeDtypeStruct(s, k) for s, k in outs],
        in_specs=[smem] + [pl.BlockSpec(memory_space=space)] * n_in,
        out_specs=[vmem] * len(outs),
        scratch_shapes=list(scratch),
        compiler_params=PARAMS,
    )


def by_quarter(kernel, in_specs, out_specs, out_shape, scratch=()):
    return pl.pallas_call(
        kernel,
        grid=(HEADS // QH,),
        in_specs=in_specs,
        out_specs=out_specs,
        out_shape=out_shape,
        scratch_shapes=list(scratch),
        compiler_params=PARAMS,
    )


def core_pairs(n):
    return [(i, i ^ 1) for i in range(n)]


def chip_pairs(n, k):
    return [(i, i ^ (2 * k)) for i in range(n)]


def group_pairs(n, k):
    pairs = [(i, i ^ (8 * k)) for i in range(n)]
    return [(i, j) for i, j in pairs if (j > i) == (i % 2 == 1)]


def partners(value, axis, k):
    n = lax.axis_size(axis)
    return lax.ppermute(value, axis, [(i, i ^ k) for i in range(n) if i ^ k < n])


def shards(inputs, grad_out, input_map, output_map, step_size, log_decay, skip_gain):
    n = lax.axis_size("ctx")
    me = lax.axis_index("ctx")
    x, g = inputs[0], grad_out[0]
    b, c = input_map[0], output_map[0]
    steps, logs = step_size[0], log_decay[0]
    where = jnp.stack([me % 2, me // 8, (me // 2) % 4]).astype(jnp.int32)
    gains = jnp.repeat(skip_gain, PH)[None]
    groups = [[8 * j + 2 * i + core for i in range(4)] for j in range(n // 8) for core in range(2)]
    slab_inputs = (x, g, b, c, steps, logs)

    def states(own):
        if own:
            scratch, space = (), pltpu.VMEM
        else:
            scratch = [pltpu.VMEM(v.shape, v.dtype) for v in slab_inputs] + [pltpu.SemaphoreType.DMA((6,))]
            space = pltpu.HBM
        kernel = lambda *refs: states_kernel(own, *refs)
        return call(kernel, [((FEATS + SIDE, NS), F32)], 6, space, scratch)(where, *slab_inputs)[0]

    send = states(False)
    first = lax.ppermute(send, "ctx", core_pairs(n))
    own = states(True)
    parts = call(chip_kernel, [((PIECE, NS), F32)] * 4, 2)(where, first, own)
    mine = [parts[0]] + [lax.ppermute(parts[k], "ctx", chip_pairs(n, k)) for k in range(1, 4)]

    cols = pl.BlockSpec((TOK, QR), lambda i: (0, i))
    rows = pl.BlockSpec((QH, TOK), lambda i: (i, 0))
    fixed = lambda r, l: pl.BlockSpec((r, l), lambda i: (0, 0))
    wide = jax.ShapeDtypeStruct((TOK, FEATS), F32)
    within, back, maps = by_quarter(
        slab_kernel,
        [cols, cols, fixed(TOK, NS), fixed(TOK, NS), rows, rows, fixed(8, NS)],
        [cols, cols, fixed(TOK, 2 * NS)],
        [wide, wide, jax.ShapeDtypeStruct((TOK, 2 * NS), F32)],
        [pltpu.VMEM((TOK, TOK), F32)],
    )(*slab_inputs, parts[0])

    total, placed = call(group_kernel, [((PIECE, NS), F32), ((4 * PIECE, NS), F32)], 4)(where, *mine)
    tops = [lax.ppermute(total, "ctx", group_pairs(n, k)) for k in range(1, 4)]
    tops[-1], within, back, maps = lax.optimization_barrier((tops[-1], within, back, maps))
    (ready,) = call(prefix_kernel, [((4 * NEAR, NS), F32)], 4)(where, placed, *tops)
    near = lax.all_to_all(ready, "ctx", 0, 0, axis_index_groups=groups, tiled=True)
    far = lax.ppermute(near, "ctx", core_pairs(n))
    (near_maps,) = call(near_maps_kernel, [((TOK, NS), F32)], 6)(where, x, g, steps, logs, near, first)
    maps, skips = call(far_maps_kernel, [((TOK, 2 * NS), F32), ((HEADS, NS), F32)], 8)(
        where, x, g, steps, logs, near, far, maps, near_maps
    )
    tp = lax.axis_size("tp")
    swapped = lax.all_to_all(maps.reshape(tp, TOK // tp, 2 * NS), "tp", 0, 0)
    outs = [((TOK, FEATS), BF16)] * 2 + [((HEADS, TOK), F32)] * 2
    mixed, ginputs, gstep, gdecay = call(cross_kernel, outs, 14)(
        where, x, g, within, back, steps, logs, gains, b, c, near, far, first, send, own
    )
    reduced = jnp.sum(swapped, axis=0)
    skip = skips[:, 0]
    skip_total = skip + partners(skip, "dp", 1) + partners(skip, "dp", 2) + partners(skip, "dp", 3)
    factor = 1.0 / math.sqrt(lax.axis_size("dp") * TOK * n * PH)
    return (
        mixed[None],
        ginputs[None],
        gstep[None],
        gdecay[None],
        reduced[None, :, :NS],
        reduced[None, :, NS:],
        skip_total * factor,
    )


def solution(mesh):
    in_specs = (
        P("dp", "ctx", "tp"),
        P("dp", "ctx", "tp"),
        P("dp", "ctx", None),
        P("dp", "ctx", None),
        P("dp", "tp", "ctx"),
        P("dp", "tp", "ctx"),
        P("tp"),
    )
    out_specs = (
        P("dp", "ctx", "tp"),
        P("dp", "ctx", "tp"),
        P("dp", "tp", "ctx"),
        P("dp", "tp", "ctx"),
        P("dp", ("ctx", "tp"), None),
        P("dp", ("ctx", "tp"), None),
        P("tp"),
    )
    return jax.shard_map(shards, mesh=mesh, in_specs=in_specs, out_specs=out_specs, check_vma=False)
```

```python
import math

import jax
import jax.numpy as jnp
from jax import lax
from jax.experimental import pallas as pl
from jax.experimental.pallas import tpu as pltpu
from jax.sharding import PartitionSpec as P

F32 = jnp.float32
BF16 = jnp.bfloat16
HIGHEST = lax.Precision.HIGHEST
TOK = 128
HEADS = 32
PH = 64
NS = 128
FEATS = HEADS * PH
QH = 8
QR = QH * PH
PIECE = QR + 2 * QH
NEAR = QR + QH
SIDE = 2 * HEADS
VMEM_LIMIT = 48 * 1024 * 1024


def iota(shape, dim):
    return lax.broadcasted_iota(jnp.int32, shape, dim)


def split(value):
    high = value.astype(BF16)
    low = (value - high.astype(F32)).astype(BF16)
    return high, low


def dot(a, b, ca, cb, precision=None):
    return lax.dot_general(a, b, (((ca,), (cb,)), ((), ())), preferred_element_type=F32, precision=precision)


def running_sum(logs):
    upto = (iota((TOK, TOK), 0) <= iota((TOK, TOK), 1)).astype(F32)
    return dot(logs, upto, 1, 0, HIGHEST)


def expander(heads, first, width):
    row = iota((2 * heads, width), 0)
    row = jnp.where(row >= heads, row - heads, row)
    return (row == (iota((2 * heads, width), 1) + first) // PH).astype(F32).astype(BF16)


def spread_heads(factors, first, width):
    high, low = split(factors.T)
    return dot(jnp.concatenate([high, low], axis=1), expander(factors.shape[0], first, width), 1, 0)


def gate(flag, value):
    return jnp.where(flag, value, 0.0)


def fetch(refs, held, sems):
    copies = [pltpu.make_async_copy(ref, slot, sems.at[i]) for i, (ref, slot) in enumerate(zip(refs, held, strict=True))]
    for copy in copies:
        copy.start()
    for copy in copies:
        copy.wait()


def states_kernel(own, where_ref, *refs):
    out_ref, held = refs[6], refs[7:13]
    fetch(refs[:6], held, refs[13])
    x_ref, g_ref, b_ref, c_ref, step_ref, log_ref = held
    cum = running_sum(log_ref[...])

    def summed(values_ref, factors, map_ref):
        doubled = jnp.concatenate([map_ref[...], map_ref[...]], axis=0)
        for first in range(0, FEATS, QR):
            weighted = values_ref[:, first : first + QR].astype(F32) * spread_heads(factors, first, QR)
            high, low = split(weighted)
            out_ref[first : first + QR, :] = dot(jnp.concatenate([high, low], axis=0), doubled, 0, 0)

    forward = where_ref[0] == (1 if own else 0)

    @pl.when(forward)
    def _():
        summed(x_ref, step_ref[...] * jnp.exp(cum[:, TOK - 1 : TOK] - cum), b_ref)

    @pl.when(jnp.logical_not(forward))
    def _():
        summed(g_ref, jnp.exp(cum), c_ref)

    out_ref[FEATS : FEATS + HEADS, :] = jnp.broadcast_to(cum[:, TOK - 1 : TOK], (HEADS, NS))
    products = jnp.sum(x_ref[...].astype(F32) * g_ref[...].astype(F32), axis=0, keepdims=True)
    owner = (iota((HEADS, FEATS), 1) // PH == iota((HEADS, FEATS), 0)).astype(F32)
    skips = jnp.sum(owner * products, axis=1, keepdims=True)
    out_ref[FEATS + HEADS : FEATS + SIDE, :] = jnp.broadcast_to(skips, (HEADS, NS))


def chip_kernel(where_ref, got_ref, own_ref, *out_refs):
    place = where_ref[2]
    for k, out_ref in enumerate(out_refs):
        quarter = jnp.bitwise_xor(place, k)
        rows = pl.ds(pl.multiple_of(FEATS + quarter * QH, QH), QH)
        logs, got_logs = own_ref[rows, :], got_ref[rows, :]
        decay = jnp.exp(logs)
        for j in range(QH):
            rows = pl.ds(pl.multiple_of(quarter * QR + j * PH, PH), PH)
            out_ref[j * PH : (j + 1) * PH, :] = decay[j : j + 1, :] * got_ref[rows, :] + own_ref[rows, :]
        out_ref[QR : QR + QH, :] = logs + got_logs
        rows = pl.ds(pl.multiple_of(FEATS + HEADS + quarter * QH, QH), QH)
        out_ref[QR + QH : PIECE, :] = own_ref[rows, :] + got_ref[rows, :]


def group_kernel(where_ref, *refs):
    got, out_ref, parts_ref = refs[:4], refs[4], refs[5]
    forward = where_ref[0] == 1
    place = where_ref[2]
    for k in range(4):
        parts_ref[pl.ds(pl.multiple_of(jnp.bitwise_xor(place, k) * PIECE, 8), PIECE), :] = got[k][...]
    logs = [parts_ref[k * PIECE + QR : k * PIECE + QR + QH, :] for k in range(4)]
    none = jnp.zeros_like(logs[0])
    weights = [jnp.exp(jnp.where(forward, sum(logs[k + 1 :], none), sum(logs[:k], none))) for k in range(4)]
    for j in range(QH):
        terms = [
            weights[k][j : j + 1, :] * parts_ref[k * PIECE + j * PH : k * PIECE + (j + 1) * PH, :] for k in range(4)
        ]
        out_ref[j * PH : (j + 1) * PH, :] = (terms[0] + terms[1]) + (terms[2] + terms[3])
    side = [parts_ref[k * PIECE + QR : (k + 1) * PIECE, :] for k in range(4)]
    out_ref[QR:PIECE, :] = (side[0] + side[1]) + (side[2] + side[3])


def prefix_kernel(where_ref, parts_ref, *refs):
    forward = where_ref[0] == 1
    me = where_ref[1]
    group = [jnp.bitwise_xor(me, k) for k in range(4)]
    group = [jnp.where(forward, p, 3 - p) for p in group]
    tops, out_ref = refs[:3], refs[3]
    top_logs = [t[QR : QR + QH, :] for t in tops]
    weights = []
    for k in range(3):
        between = [
            gate((group[k + 1] < group[i + 1]) & (group[i + 1] < group[0]), top_logs[i]) for i in range(3) if i != k
        ]
        weights.append(jnp.exp(between[0] + between[1]))
    decays = [jnp.exp(parts_ref[k * PIECE + QR : k * PIECE + QR + QH, :]) for k in range(4)]

    def scan(sequence, carries_own):
        for j in range(QH):
            rows = slice(j * PH, (j + 1) * PH)
            at = slice(j, j + 1)
            state = weights[0][at, :] * tops[0][rows, :] + weights[1][at, :] * tops[1][rows, :]
            state = state + weights[2][at, :] * tops[2][rows, :]
            for k in sequence:
                out_ref[k * NEAR + j * PH : k * NEAR + (j + 1) * PH, :] = state
                if k != sequence[-1]:
                    state = decays[k][at, :] * state + parts_ref[k * PIECE + j * PH : k * PIECE + (j + 1) * PH, :]
        skips = tops[0][QR + QH :, :] + tops[1][QR + QH :, :] + tops[2][QR + QH :, :]
        if carries_own:
            for k in range(4):
                skips = skips + parts_ref[k * PIECE + QR + QH : (k + 1) * PIECE, :]
        for k in range(4):
            out_ref[k * NEAR + QR : (k + 1) * NEAR, :] = skips

    @pl.when(forward)
    def _():
        scan((0, 1, 2, 3), True)

    @pl.when(jnp.logical_not(forward))
    def _():
        scan((3, 2, 1, 0), False)


def slab_kernel(x_ref, g_ref, b_ref, c_ref, step_ref, log_ref, after_ref, within_ref, back_ref, maps_ref, summed):
    quarter = pl.program_id(0)

    @pl.when(quarter == 0)
    def _():
        summed[...] = jnp.zeros_like(summed)

    affinity = dot(c_ref[...], b_ref[...], 1, 1)
    causal = iota((TOK, TOK), 0) >= iota((TOK, TOK), 1)
    cum = running_sum(log_ref[...])
    columns = cum.T
    left = iota((TOK, 2 * PH), 1) < PH
    zero = jnp.zeros((TOK, 2 * PH), BF16)
    for pair in range(QH // 2):
        lanes = slice(pair * 2 * PH, (pair + 1) * 2 * PH)
        x, g = x_ref[:, lanes], g_ref[:, lanes]
        xs = (jnp.where(left, x, zero), jnp.where(left, zero, x))
        gs = (jnp.where(left, g, zero), jnp.where(left, zero, g))
        mixes = []
        for side in range(2):
            j = 2 * pair + side
            gap = columns[:, j : j + 1] - cum[j : j + 1, :]
            decays = jnp.exp(jnp.where(causal, gap, -1e30)) * step_ref[j : j + 1, :]
            summed[...] += decays * dot(gs[side], x, 1, 1)
            mixes.extend(split(affinity * decays))
        within_ref[:, lanes] = dot(
            jnp.concatenate(mixes, axis=1), jnp.concatenate([xs[0], xs[0], xs[1], xs[1]], axis=0), 1, 0
        )
        back_ref[:, lanes] = dot(
            jnp.concatenate(mixes, axis=0), jnp.concatenate([gs[0], gs[0], gs[1], gs[1]], axis=0), 0, 0
        )

    @pl.when(quarter == pl.num_programs(0) - 1)
    def _():
        high, low = split(summed[...])
        b, c = b_ref[...], c_ref[...]
        maps_ref[:, :NS] = dot(jnp.concatenate([high, low], axis=0), jnp.concatenate([c, c], axis=0), 0, 0)
        maps_ref[:, NS:] = dot(jnp.concatenate([high, low], axis=1), jnp.concatenate([b, b], axis=0), 1, 0)


def at_slab(quarter, near_ref, first_ref):
    decay = jnp.exp(first_ref[FEATS + quarter * QH : FEATS + (quarter + 1) * QH, :])
    slots = []
    for j in range(QH):
        near = near_ref[quarter * NEAR + j * PH : quarter * NEAR + (j + 1) * PH, :]
        first = quarter * QR + j * PH
        slots.append(decay[j : j + 1, :] * near + first_ref[first : first + PH, :])
    return jnp.concatenate(slots, axis=0)


def weights_kernel(where_ref, x_ref, g_ref, step_ref, log_ref, after_ref, *out_refs):
    forward = where_ref[0] == 1
    cum = running_sum(log_ref[...])
    starts = jnp.exp(cum)
    sources = step_ref[...] * jnp.exp(cum[:, TOK - 1 : TOK] - cum)
    for scanned, high_ref, low_ref in ((forward, *out_refs[:2]), (jnp.logical_not(forward), *out_refs[2:])):
        factors = jnp.where(scanned, starts, sources)
        for quarter in range(4):
            lanes = slice(quarter * QR, (quarter + 1) * QR)
            values = jnp.where(scanned, g_ref[:, lanes].astype(F32), x_ref[:, lanes].astype(F32))
            high_ref[:, lanes], low_ref[:, lanes] = split(values * spread_heads(factors, quarter * QR, QR))


def weighted_sum(high_ref, low_ref, state_of):
    total = jnp.zeros((TOK, NS), F32)
    for quarter in range(4):
        lanes = slice(quarter * QR, (quarter + 1) * QR)
        high, low = high_ref[:, lanes], low_ref[:, lanes]
        state_high, state_low = split(state_of(quarter))
        total = total + (dot(high, state_high, 1, 0) + (dot(low, state_high, 1, 0) + dot(high, state_low, 1, 0)))
    return total


def near_maps_kernel(where_ref, high_far, low_far, near_ref, first_ref, out_ref, high_ref, low_ref, sems):
    fetch((high_far, low_far), (high_ref, low_ref), sems)
    out_ref[...] = weighted_sum(high_ref, low_ref, lambda quarter: at_slab(quarter, near_ref, first_ref))


def far_maps_kernel(where_ref, high_ref, low_ref, near_ref, far_ref, maps_in_ref, near_maps_ref, maps_ref, skip_ref):
    forward = where_ref[0] == 1
    other = weighted_sum(high_ref, low_ref, lambda quarter: far_ref[quarter * NEAR : quarter * NEAR + QR, :])
    for quarter in range(4):
        side = slice(quarter * NEAR + QR, (quarter + 1) * NEAR)
        skip_ref[quarter * QH : (quarter + 1) * QH, :] = near_ref[side, :] + far_ref[side, :]
    mine = near_maps_ref[...]
    maps_ref[:, :NS] = maps_in_ref[:, :NS] + jnp.where(forward, other, mine)
    maps_ref[:, NS:] = maps_in_ref[:, NS:] + jnp.where(forward, mine, other)


def cross_kernel(
    where_ref, within_far, back_far, x_ref, g_ref, step_ref, log_ref, gain_ref, b_ref, c_ref,
    near_ref, far_ref, first_ref,
    mixed_ref, ginputs_ref, gstep_ref, gdecay_ref,
    within_ref, back_ref, sems,
):
    copies = []
    for quarter in range(4):
        lanes = slice(quarter * QR, (quarter + 1) * QR)
        pairs = ((within_far, within_ref), (back_far, back_ref))
        copies.append(
            [
                pltpu.make_async_copy(source.at[:, lanes], slot.at[:, lanes], sems.at[quarter, i])
                for i, (source, slot) in enumerate(pairs)
            ]
        )
        for copy in copies[-1]:
            copy.start()
    forward = where_ref[0] == 1
    cums = running_sum(log_ref[...])
    b, c = b_ref[...], c_ref[...]
    two_b, two_c = jnp.concatenate([b, b], axis=1), jnp.concatenate([c, c], axis=1)
    owner = (iota((QR, QH), 0) // PH == iota((QR, QH), 1)).astype(F32).astype(BF16)
    doubled = jnp.concatenate([owner, owner], axis=0)
    heads_of = (iota((QH, QR), 1) // PH == iota((QH, QR), 0)).astype(F32)
    after = (iota((TOK, TOK), 0) >= iota((TOK, TOK), 1)).astype(F32)

    def by_head(values):
        return dot(jnp.concatenate(split(values), axis=1), doubled, 1, 0).T

    for quarter in range(4):
        lanes = slice(quarter * QR, (quarter + 1) * QR)
        heads = slice(quarter * QH, (quarter + 1) * QH)
        cum, steps = cums[heads, :], step_ref[heads, :]
        through = jnp.exp(cum[:, TOK - 1 : TOK])
        scanned = at_slab(quarter, near_ref, first_ref)
        other = far_ref[quarter * NEAR : quarter * NEAR + QR, :]
        ent = jnp.where(forward, scanned, other)
        arr = jnp.where(forward, other, scanned)
        for copy in copies[quarter]:
            copy.wait()
        x, g = x_ref[:, lanes].astype(F32), g_ref[:, lanes].astype(F32)
        starts = spread_heads(jnp.exp(cum), 0, QR)
        sources = spread_heads(steps * jnp.exp(cum[:, TOK - 1 : TOK] - cum), 0, QR)
        output = within_ref[:, lanes] + dot(two_c, jnp.concatenate(split(ent), axis=1), 1, 1) * starts
        later = dot(two_b, jnp.concatenate(split(arr), axis=1), 1, 1) * sources
        back = back_ref[:, lanes] + later
        gain = gain_ref[:, lanes]
        mixed_ref[:, lanes] = (output + gain * x).astype(BF16)
        ginputs_ref[:, lanes] = (back + gain * g).astype(BF16)
        steps_part = x * back
        gstep_ref[heads, :] = by_head(steps_part) / steps
        change = by_head(g * output - steps_part)
        local = jnp.sum(heads_of * jnp.sum(x * later, axis=0, keepdims=True), axis=1, keepdims=True)
        carried = [
            jnp.sum(arr[j * PH : (j + 1) * PH, :] * ent[j * PH : (j + 1) * PH, :], axis=0, keepdims=True)
            for j in range(QH)
        ]
        edge = local + through * jnp.sum(jnp.concatenate(carried, axis=0), axis=1, keepdims=True)
        change = change + jnp.where(iota((QH, TOK), 1) == TOK - 1, edge, 0.0)
        gdecay_ref[heads, :] = dot(change, after, 1, 0, HIGHEST)


PARAMS = pltpu.CompilerParams(vmem_limit_bytes=VMEM_LIMIT)


def call(kernel, outs, n_in, n_far=0, scratch=()):
    smem = pl.BlockSpec(memory_space=pltpu.SMEM)
    vmem = pl.BlockSpec(memory_space=pltpu.VMEM)
    run = pl.pallas_call(
        kernel,
        out_shape=[jax.ShapeDtypeStruct(s, k) for s, k in outs],
        in_specs=[smem] + [pl.BlockSpec(memory_space=pltpu.HBM)] * n_far + [vmem] * n_in,
        out_specs=[vmem] * len(outs),
        scratch_shapes=list(scratch),
        compiler_params=PARAMS,
    )

    def place(where, *arrays):
        far = [pltpu.with_memory_space_constraint(v, pltpu.HBM) for v in arrays[:n_far]]
        return run(where, *far, *arrays[n_far:])

    return place


def by_quarter(kernel, in_specs, out_specs, out_shape, scratch=()):
    return pl.pallas_call(
        kernel,
        grid=(HEADS // QH,),
        in_specs=in_specs,
        out_specs=out_specs,
        out_shape=out_shape,
        scratch_shapes=list(scratch),
        compiler_params=PARAMS,
    )


def core_pairs(n):
    return [(i, i ^ 1) for i in range(n)]


def chip_pairs(n, k):
    return [(i, i ^ (2 * k)) for i in range(n)]


def group_pairs(n, k):
    pairs = [(i, i ^ (8 * k)) for i in range(n)]
    return [(i, j) for i, j in pairs if (j > i) == (i % 2 == 1)]


def partners(value, axis, k):
    n = lax.axis_size(axis)
    return lax.ppermute(value, axis, [(i, i ^ k) for i in range(n) if i ^ k < n])


def shards(inputs, grad_out, input_map, output_map, step_size, log_decay, skip_gain):
    n = lax.axis_size("ctx")
    me = lax.axis_index("ctx")
    x, g = inputs[0], grad_out[0]
    b, c = input_map[0], output_map[0]
    steps, logs = step_size[0], log_decay[0]
    where = jnp.stack([me % 2, me // 8, (me // 2) % 4]).astype(jnp.int32)
    gains = jnp.repeat(skip_gain, PH)[None]
    groups = [[8 * j + 2 * i + core for i in range(4)] for j in range(n // 8) for core in range(2)]
    slab_inputs = (x, g, b, c, steps, logs)

    def states(own):
        scratch = [pltpu.VMEM(v.shape, v.dtype) for v in slab_inputs] + [pltpu.SemaphoreType.DMA((6,))]
        kernel = lambda *refs: states_kernel(own, *refs)
        return call(kernel, [((FEATS + SIDE, NS), F32)], 0, 6, scratch)(where, *slab_inputs)[0]

    send = states(False)
    first = lax.ppermute(send, "ctx", core_pairs(n))
    own = states(True)
    parts = list(call(chip_kernel, [((PIECE, NS), F32)] * 4, 2)(where, first, own))
    *slab_inputs, parts[0] = lax.optimization_barrier((*slab_inputs, parts[0]))
    x, g, b, c, steps, logs = slab_inputs
    mine = [parts[0]] + [lax.ppermute(parts[k], "ctx", chip_pairs(n, k)) for k in range(1, 4)]

    cols = pl.BlockSpec((TOK, QR), lambda i: (0, i))
    rows = pl.BlockSpec((QH, TOK), lambda i: (i, 0))
    fixed = lambda r, l: pl.BlockSpec((r, l), lambda i: (0, 0))
    wide = jax.ShapeDtypeStruct((TOK, FEATS), F32)
    within, back, maps = by_quarter(
        slab_kernel,
        [cols, cols, fixed(TOK, NS), fixed(TOK, NS), rows, rows, fixed(8, NS)],
        [cols, cols, fixed(TOK, 2 * NS)],
        [wide, wide, jax.ShapeDtypeStruct((TOK, 2 * NS), F32)],
        [pltpu.VMEM((TOK, TOK), F32)],
    )(*slab_inputs, parts[0])

    total, placed = call(group_kernel, [((PIECE, NS), F32), ((4 * PIECE, NS), F32)], 4)(where, *mine)
    tops = [lax.ppermute(total, "ctx", group_pairs(n, k)) for k in range(1, 4)]
    weights = call(weights_kernel, [((TOK, FEATS), BF16)] * 4, 5)(where, x, g, steps, logs, parts[0])
    tops[-1], within, back, maps, *weights = lax.optimization_barrier((tops[-1], within, back, maps, *weights))
    (ready,) = call(prefix_kernel, [((4 * NEAR, NS), F32)], 4)(where, placed, *tops)
    near = lax.all_to_all(ready, "ctx", 0, 0, axis_index_groups=groups, tiled=True)
    far = lax.ppermute(near, "ctx", core_pairs(n))
    halves = [pltpu.VMEM((TOK, FEATS), BF16)] * 2 + [pltpu.SemaphoreType.DMA((2,))]
    (near_maps,) = call(near_maps_kernel, [((TOK, NS), F32)], 2, 2, halves)(where, *weights[:2], near, first)
    maps, skips = call(far_maps_kernel, [((TOK, 2 * NS), F32), ((HEADS, NS), F32)], 6)(
        where, *weights[2:], near, far, maps, near_maps
    )
    tp = lax.axis_size("tp")
    swapped = lax.all_to_all(maps.reshape(tp, TOK // tp, 2 * NS), "tp", 0, 0)
    slots = [pltpu.VMEM((TOK, FEATS), F32)] * 2 + [pltpu.SemaphoreType.DMA((4, 2))]
    outs = [((TOK, FEATS), BF16)] * 2 + [((HEADS, TOK), F32)] * 2
    mixed, ginputs, gstep, gdecay = call(cross_kernel, outs, 10, 2, slots)(
        where, within, back, x, g, steps, logs, gains, b, c, near, far, first
    )
    reduced = jnp.sum(swapped, axis=0)
    skip = skips[:, 0]
    skip_total = skip + partners(skip, "dp", 1) + partners(skip, "dp", 2) + partners(skip, "dp", 3)
    factor = 1.0 / math.sqrt(lax.axis_size("dp") * TOK * n * PH)
    return (
        mixed[None],
        ginputs[None],
        gstep[None],
        gdecay[None],
        reduced[None, :, :NS],
        reduced[None, :, NS:],
        skip_total * factor,
    )


def solution(mesh):
    in_specs = (
        P("dp", "ctx", "tp"),
        P("dp", "ctx", "tp"),
        P("dp", "ctx", None),
        P("dp", "ctx", None),
        P("dp", "tp", "ctx"),
        P("dp", "tp", "ctx"),
        P("tp"),
    )
    out_specs = (
        P("dp", "ctx", "tp"),
        P("dp", "ctx", "tp"),
        P("dp", "tp", "ctx"),
        P("dp", "tp", "ctx"),
        P("dp", ("ctx", "tp"), None),
        P("dp", ("ctx", "tp"), None),
        P("tp"),
    )
    return jax.shard_map(shards, mesh=mesh, in_specs=in_specs, out_specs=out_specs, check_vma=False)
```

```python
import math

import jax
import jax.numpy as jnp
from jax import lax
from jax.experimental import pallas as pl
from jax.experimental.pallas import tpu as pltpu
from jax.sharding import PartitionSpec as P

F32 = jnp.float32
BF16 = jnp.bfloat16
HIGHEST = lax.Precision.HIGHEST
TOK = 128
HEADS = 32
PH = 64
NS = 128
FEATS = HEADS * PH
QH = 8
QR = QH * PH
PIECE = QR + QH
TOP = PIECE + QH
NEAR = QR + QH
SIDE = HEADS
VMEM_LIMIT = 48 * 1024 * 1024


def iota(shape, dim):
    return lax.broadcasted_iota(jnp.int32, shape, dim)


def split(value):
    high = value.astype(BF16)
    low = (value - high.astype(F32)).astype(BF16)
    return high, low


def dot(a, b, ca, cb, precision=None):
    return lax.dot_general(a, b, (((ca,), (cb,)), ((), ())), preferred_element_type=F32, precision=precision)


def running_sum(logs):
    upto = (iota((TOK, TOK), 0) <= iota((TOK, TOK), 1)).astype(F32)
    return dot(logs, upto, 1, 0, HIGHEST)


def expander(heads, first, width):
    row = iota((2 * heads, width), 0)
    row = jnp.where(row >= heads, row - heads, row)
    return (row == (iota((2 * heads, width), 1) + first) // PH).astype(F32).astype(BF16)


def spread_heads(factors, first, width):
    high, low = split(factors.T)
    return dot(jnp.concatenate([high, low], axis=1), expander(factors.shape[0], first, width), 1, 0)


def gate(flag, value):
    return jnp.where(flag, value, 0.0)


def fetch(refs, held, sems):
    copies = [pltpu.make_async_copy(ref, slot, sems.at[i]) for i, (ref, slot) in enumerate(zip(refs, held, strict=True))]
    for copy in copies:
        copy.start()
    for copy in copies:
        copy.wait()


def states_kernel(own, where_ref, *refs):
    out_ref, skip_ref, held = refs[6], refs[7] if own else None, refs[-7:-1]
    fetch(refs[:6], held, refs[-1])
    x_ref, g_ref, b_ref, c_ref, step_ref, log_ref = held
    cum = running_sum(log_ref[...])

    def summed(values_ref, factors, map_ref):
        doubled = jnp.concatenate([map_ref[...], map_ref[...]], axis=0)
        for first in range(0, FEATS, QR):
            weighted = values_ref[:, first : first + QR].astype(F32) * spread_heads(factors, first, QR)
            high, low = split(weighted)
            out_ref[first : first + QR, :] = dot(jnp.concatenate([high, low], axis=0), doubled, 0, 0)

    forward = where_ref[0] == (1 if own else 0)

    @pl.when(forward)
    def _():
        summed(x_ref, step_ref[...] * jnp.exp(cum[:, TOK - 1 : TOK] - cum), b_ref)

    @pl.when(jnp.logical_not(forward))
    def _():
        summed(g_ref, jnp.exp(cum), c_ref)

    out_ref[FEATS : FEATS + HEADS, :] = jnp.broadcast_to(cum[:, TOK - 1 : TOK], (HEADS, NS))
    if own:
        products = jnp.sum(x_ref[...].astype(F32) * g_ref[...].astype(F32), axis=0, keepdims=True)
        owner = (iota((HEADS, FEATS), 1) // PH == iota((HEADS, FEATS), 0)).astype(F32)
        sums = jnp.sum(owner * products, axis=1, keepdims=True)
        lane = iota((QH, NS), 1) // 32
        tile = jnp.where(lane == 0, sums[:QH, :], 0.0)
        for quarter in range(1, 4):
            tile = jnp.where(lane == quarter, sums[quarter * QH : (quarter + 1) * QH, :], tile)
        skip_ref[...] = tile


def chip_kernel(where_ref, got_ref, own_ref, *out_refs):
    place = where_ref[2]
    for k, out_ref in enumerate(out_refs):
        quarter = jnp.bitwise_xor(place, k)
        rows = pl.ds(pl.multiple_of(FEATS + quarter * QH, QH), QH)
        logs, got_logs = own_ref[rows, :], got_ref[rows, :]
        decay = jnp.exp(logs)
        for j in range(QH):
            rows = pl.ds(pl.multiple_of(quarter * QR + j * PH, PH), PH)
            out_ref[j * PH : (j + 1) * PH, :] = decay[j : j + 1, :] * got_ref[rows, :] + own_ref[rows, :]
        out_ref[QR : QR + QH, :] = logs + got_logs


def group_kernel(where_ref, *refs):
    got, skip_ref, out_ref, parts_ref = refs[:4], refs[4], refs[5], refs[6]
    forward = where_ref[0] == 1
    place = where_ref[2]
    for k in range(4):
        parts_ref[pl.ds(pl.multiple_of(jnp.bitwise_xor(place, k) * PIECE, 8), PIECE), :] = got[k][...]
    logs = [parts_ref[k * PIECE + QR : k * PIECE + QR + QH, :] for k in range(4)]
    none = jnp.zeros_like(logs[0])
    weights = [jnp.exp(jnp.where(forward, sum(logs[k + 1 :], none), sum(logs[:k], none))) for k in range(4)]
    for j in range(QH):
        terms = [
            weights[k][j : j + 1, :] * parts_ref[k * PIECE + j * PH : k * PIECE + (j + 1) * PH, :] for k in range(4)
        ]
        out_ref[j * PH : (j + 1) * PH, :] = (terms[0] + terms[1]) + (terms[2] + terms[3])
    side = [parts_ref[k * PIECE + QR : (k + 1) * PIECE, :] for k in range(4)]
    out_ref[QR:PIECE, :] = (side[0] + side[1]) + (side[2] + side[3])
    out_ref[PIECE:TOP, :] = skip_ref[...]


def prefix_kernel(where_ref, parts_ref, skip_ref, *refs):
    forward = where_ref[0] == 1
    me = where_ref[1]
    group = [jnp.bitwise_xor(me, k) for k in range(4)]
    group = [jnp.where(forward, p, 3 - p) for p in group]
    tops, out_ref = refs[:3], refs[3]
    top_logs = [t[QR : QR + QH, :] for t in tops]
    weights = []
    for k in range(3):
        between = [
            gate((group[k + 1] < group[i + 1]) & (group[i + 1] < group[0]), top_logs[i]) for i in range(3) if i != k
        ]
        weights.append(jnp.exp(between[0] + between[1]))
    decays = [jnp.exp(parts_ref[k * PIECE + QR : k * PIECE + QR + QH, :]) for k in range(4)]

    def scan(sequence, carries_own):
        for j in range(QH):
            rows = slice(j * PH, (j + 1) * PH)
            at = slice(j, j + 1)
            state = weights[0][at, :] * tops[0][rows, :] + weights[1][at, :] * tops[1][rows, :]
            state = state + weights[2][at, :] * tops[2][rows, :]
            for k in sequence:
                out_ref[k * NEAR + j * PH : k * NEAR + (j + 1) * PH, :] = state
                if k != sequence[-1]:
                    state = decays[k][at, :] * state + parts_ref[k * PIECE + j * PH : k * PIECE + (j + 1) * PH, :]
        skips = tops[0][PIECE:, :] + tops[1][PIECE:, :] + tops[2][PIECE:, :]
        if carries_own:
            skips = skips + skip_ref[...]
        for k in range(4):
            out_ref[k * NEAR + QR : (k + 1) * NEAR, :] = skips

    @pl.when(forward)
    def _():
        scan((0, 1, 2, 3), True)

    @pl.when(jnp.logical_not(forward))
    def _():
        scan((3, 2, 1, 0), False)


def slab_kernel(x_ref, g_ref, b_ref, c_ref, step_ref, log_ref, after_ref, within_ref, back_ref, maps_ref, summed):
    quarter = pl.program_id(0)

    @pl.when(quarter == 0)
    def _():
        summed[...] = jnp.zeros_like(summed)

    affinity = dot(c_ref[...], b_ref[...], 1, 1)
    causal = iota((TOK, TOK), 0) >= iota((TOK, TOK), 1)
    cum = running_sum(log_ref[...])
    columns = cum.T
    left = iota((TOK, 2 * PH), 1) < PH
    zero = jnp.zeros((TOK, 2 * PH), BF16)
    for pair in range(QH // 2):
        lanes = slice(pair * 2 * PH, (pair + 1) * 2 * PH)
        x, g = x_ref[:, lanes], g_ref[:, lanes]
        xs = (jnp.where(left, x, zero), jnp.where(left, zero, x))
        gs = (jnp.where(left, g, zero), jnp.where(left, zero, g))
        mixes = []
        for side in range(2):
            j = 2 * pair + side
            gap = columns[:, j : j + 1] - cum[j : j + 1, :]
            decays = jnp.exp(jnp.where(causal, gap, -1e30)) * step_ref[j : j + 1, :]
            summed[...] += decays * dot(gs[side], x, 1, 1)
            mixes.extend(split(affinity * decays))
        within_ref[:, lanes] = dot(
            jnp.concatenate(mixes, axis=1), jnp.concatenate([xs[0], xs[0], xs[1], xs[1]], axis=0), 1, 0
        )
        back_ref[:, lanes] = dot(
            jnp.concatenate(mixes, axis=0), jnp.concatenate([gs[0], gs[0], gs[1], gs[1]], axis=0), 0, 0
        )

    @pl.when(quarter == pl.num_programs(0) - 1)
    def _():
        high, low = split(summed[...])
        b, c = b_ref[...], c_ref[...]
        maps_ref[:, :NS] = dot(jnp.concatenate([high, low], axis=0), jnp.concatenate([c, c], axis=0), 0, 0)
        maps_ref[:, NS:] = dot(jnp.concatenate([high, low], axis=1), jnp.concatenate([b, b], axis=0), 1, 0)


def at_slab(quarter, near_ref, first_ref):
    decay = jnp.exp(first_ref[FEATS + quarter * QH : FEATS + (quarter + 1) * QH, :])
    slots = []
    for j in range(QH):
        near = near_ref[quarter * NEAR + j * PH : quarter * NEAR + (j + 1) * PH, :]
        first = quarter * QR + j * PH
        slots.append(decay[j : j + 1, :] * near + first_ref[first : first + PH, :])
    return jnp.concatenate(slots, axis=0)


def weights_kernel(where_ref, x_ref, g_ref, step_ref, log_ref, after_ref, *out_refs):
    forward = where_ref[0] == 1
    cum = running_sum(log_ref[...])
    starts = jnp.exp(cum)
    sources = step_ref[...] * jnp.exp(cum[:, TOK - 1 : TOK] - cum)
    for scanned, high_ref, low_ref in ((forward, *out_refs[:2]), (jnp.logical_not(forward), *out_refs[2:])):
        factors = jnp.where(scanned, starts, sources)
        for quarter in range(4):
            lanes = slice(quarter * QR, (quarter + 1) * QR)
            values = jnp.where(scanned, g_ref[:, lanes].astype(F32), x_ref[:, lanes].astype(F32))
            high_ref[:, lanes], low_ref[:, lanes] = split(values * spread_heads(factors, quarter * QR, QR))


def weighted_sum(high_ref, low_ref, state_of):
    total = jnp.zeros((TOK, NS), F32)
    for quarter in range(4):
        lanes = slice(quarter * QR, (quarter + 1) * QR)
        high, low = high_ref[:, lanes], low_ref[:, lanes]
        state_high, state_low = split(state_of(quarter))
        total = total + (dot(high, state_high, 1, 0) + (dot(low, state_high, 1, 0) + dot(high, state_low, 1, 0)))
    return total


def near_maps_kernel(where_ref, high_far, low_far, near_ref, first_ref, out_ref, high_ref, low_ref, sems):
    fetch((high_far, low_far), (high_ref, low_ref), sems)
    out_ref[...] = weighted_sum(high_ref, low_ref, lambda quarter: at_slab(quarter, near_ref, first_ref))


def far_maps_kernel(where_ref, high_ref, low_ref, near_ref, far_ref, maps_in_ref, near_maps_ref, maps_ref, skip_ref):
    forward = where_ref[0] == 1
    other = weighted_sum(high_ref, low_ref, lambda quarter: far_ref[quarter * NEAR : quarter * NEAR + QR, :])
    sides = [slice(quarter * NEAR + QR, (quarter + 1) * NEAR) for quarter in range(4)]
    skip_ref[...] = sum([near_ref[side, :] + far_ref[side, :] for side in sides], jnp.zeros((QH, NS), F32))
    mine = near_maps_ref[...]
    maps_ref[:, :NS] = maps_in_ref[:, :NS] + jnp.where(forward, other, mine)
    maps_ref[:, NS:] = maps_in_ref[:, NS:] + jnp.where(forward, mine, other)


def cross_kernel(
    where_ref, within_far, back_far, x_ref, g_ref, step_ref, log_ref, gain_ref, b_ref, c_ref,
    near_ref, far_ref, first_ref,
    mixed_ref, ginputs_ref, gstep_ref, gdecay_ref,
    within_ref, back_ref, sems,
):
    copies = []
    for quarter in range(4):
        lanes = slice(quarter * QR, (quarter + 1) * QR)
        pairs = ((within_far, within_ref), (back_far, back_ref))
        copies.append(
            [
                pltpu.make_async_copy(source.at[:, lanes], slot.at[:, lanes], sems.at[quarter, i])
                for i, (source, slot) in enumerate(pairs)
            ]
        )
        for copy in copies[-1]:
            copy.start()
    forward = where_ref[0] == 1
    cums = running_sum(log_ref[...])
    b, c = b_ref[...], c_ref[...]
    two_b, two_c = jnp.concatenate([b, b], axis=1), jnp.concatenate([c, c], axis=1)
    owner = (iota((QR, QH), 0) // PH == iota((QR, QH), 1)).astype(F32).astype(BF16)
    doubled = jnp.concatenate([owner, owner], axis=0)
    heads_of = (iota((QH, QR), 1) // PH == iota((QH, QR), 0)).astype(F32)
    after = (iota((TOK, TOK), 0) >= iota((TOK, TOK), 1)).astype(F32)

    def by_head(values):
        return dot(jnp.concatenate(split(values), axis=1), doubled, 1, 0).T

    for quarter in range(4):
        lanes = slice(quarter * QR, (quarter + 1) * QR)
        heads = slice(quarter * QH, (quarter + 1) * QH)
        cum, steps = cums[heads, :], step_ref[heads, :]
        through = jnp.exp(cum[:, TOK - 1 : TOK])
        scanned = at_slab(quarter, near_ref, first_ref)
        other = far_ref[quarter * NEAR : quarter * NEAR + QR, :]
        ent = jnp.where(forward, scanned, other)
        arr = jnp.where(forward, other, scanned)
        for copy in copies[quarter]:
            copy.wait()
        x, g = x_ref[:, lanes].astype(F32), g_ref[:, lanes].astype(F32)
        starts = spread_heads(jnp.exp(cum), 0, QR)
        sources = spread_heads(steps * jnp.exp(cum[:, TOK - 1 : TOK] - cum), 0, QR)
        output = within_ref[:, lanes] + dot(two_c, jnp.concatenate(split(ent), axis=1), 1, 1) * starts
        later = dot(two_b, jnp.concatenate(split(arr), axis=1), 1, 1) * sources
        back = back_ref[:, lanes] + later
        gain = gain_ref[:, lanes]
        mixed_ref[:, lanes] = (output + gain * x).astype(BF16)
        ginputs_ref[:, lanes] = (back + gain * g).astype(BF16)
        steps_part = x * back
        gstep_ref[heads, :] = by_head(steps_part) / steps
        change = by_head(g * output - steps_part)
        local = jnp.sum(heads_of * jnp.sum(x * later, axis=0, keepdims=True), axis=1, keepdims=True)
        carried = [
            jnp.sum(arr[j * PH : (j + 1) * PH, :] * ent[j * PH : (j + 1) * PH, :], axis=0, keepdims=True)
            for j in range(QH)
        ]
        edge = local + through * jnp.sum(jnp.concatenate(carried, axis=0), axis=1, keepdims=True)
        change = change + jnp.where(iota((QH, TOK), 1) == TOK - 1, edge, 0.0)
        gdecay_ref[heads, :] = dot(change, after, 1, 0, HIGHEST)


PARAMS = pltpu.CompilerParams(vmem_limit_bytes=VMEM_LIMIT)


def call(kernel, outs, n_in, n_far=0, scratch=()):
    smem = pl.BlockSpec(memory_space=pltpu.SMEM)
    vmem = pl.BlockSpec(memory_space=pltpu.VMEM)
    run = pl.pallas_call(
        kernel,
        out_shape=[jax.ShapeDtypeStruct(s, k) for s, k in outs],
        in_specs=[smem] + [pl.BlockSpec(memory_space=pltpu.HBM)] * n_far + [vmem] * n_in,
        out_specs=[vmem] * len(outs),
        scratch_shapes=list(scratch),
        compiler_params=PARAMS,
    )

    def place(where, *arrays):
        far = [pltpu.with_memory_space_constraint(v, pltpu.HBM) for v in arrays[:n_far]]
        return run(where, *far, *arrays[n_far:])

    return place


def by_quarter(kernel, in_specs, out_specs, out_shape, scratch=()):
    return pl.pallas_call(
        kernel,
        grid=(HEADS // QH,),
        in_specs=in_specs,
        out_specs=out_specs,
        out_shape=out_shape,
        scratch_shapes=list(scratch),
        compiler_params=PARAMS,
    )


def core_pairs(n):
    return [(i, i ^ 1) for i in range(n)]


def chip_pairs(n, k):
    return [(i, i ^ (2 * k)) for i in range(n)]


def group_pairs(n, k):
    pairs = [(i, i ^ (8 * k)) for i in range(n)]
    return [(i, j) for i, j in pairs if (j > i) == (i % 2 == 1)]


def partners(value, axis, k):
    n = lax.axis_size(axis)
    return lax.ppermute(value, axis, [(i, i ^ k) for i in range(n) if i ^ k < n])


def shards(inputs, grad_out, input_map, output_map, step_size, log_decay, skip_gain):
    n = lax.axis_size("ctx")
    me = lax.axis_index("ctx")
    x, g = inputs[0], grad_out[0]
    b, c = input_map[0], output_map[0]
    steps, logs = step_size[0], log_decay[0]
    where = jnp.stack([me % 2, me // 8, (me // 2) % 4]).astype(jnp.int32)
    gains = jnp.repeat(skip_gain, PH)[None]
    groups = [[8 * j + 2 * i + core for i in range(4)] for j in range(n // 8) for core in range(2)]
    slab_inputs = (x, g, b, c, steps, logs)

    def states(own):
        scratch = [pltpu.VMEM(v.shape, v.dtype) for v in slab_inputs] + [pltpu.SemaphoreType.DMA((6,))]
        kernel = lambda *refs: states_kernel(own, *refs)
        outs = [((FEATS + SIDE, NS), F32)] + ([((QH, NS), F32)] if own else [])
        return call(kernel, outs, 0, 6, scratch)(where, *slab_inputs)

    (send,) = states(False)
    first = lax.ppermute(send, "ctx", core_pairs(n))
    own, skip = states(True)
    parts = list(call(chip_kernel, [((PIECE, NS), F32)] * 4, 2)(where, first, own))
    *slab_inputs, parts[0] = lax.optimization_barrier((*slab_inputs, parts[0]))
    x, g, b, c, steps, logs = slab_inputs
    mine = [parts[0]] + [lax.ppermute(parts[k], "ctx", chip_pairs(n, k)) for k in range(1, 4)]

    cols = pl.BlockSpec((TOK, QR), lambda i: (0, i))
    rows = pl.BlockSpec((QH, TOK), lambda i: (i, 0))
    fixed = lambda r, l: pl.BlockSpec((r, l), lambda i: (0, 0))
    wide = jax.ShapeDtypeStruct((TOK, FEATS), F32)
    within, back, maps = by_quarter(
        slab_kernel,
        [cols, cols, fixed(TOK, NS), fixed(TOK, NS), rows, rows, fixed(8, NS)],
        [cols, cols, fixed(TOK, 2 * NS)],
        [wide, wide, jax.ShapeDtypeStruct((TOK, 2 * NS), F32)],
        [pltpu.VMEM((TOK, TOK), F32)],
    )(*slab_inputs, parts[0])

    mine[1], skip = lax.optimization_barrier((mine[1], skip))
    skip = skip + partners(skip, "dp", 1) + partners(skip, "dp", 2) + partners(skip, "dp", 3)
    skip = skip + lax.ppermute(skip, "ctx", core_pairs(n))
    total, placed = call(group_kernel, [((TOP, NS), F32), ((4 * PIECE, NS), F32)], 5)(where, *mine, skip)
    tops = [lax.ppermute(total, "ctx", group_pairs(n, k)) for k in range(1, 4)]
    weights = call(weights_kernel, [((TOK, FEATS), BF16)] * 4, 5)(where, x, g, steps, logs, parts[0])
    tops[-1], within, back, maps, *weights = lax.optimization_barrier((tops[-1], within, back, maps, *weights))
    (ready,) = call(prefix_kernel, [((4 * NEAR, NS), F32)], 5)(where, placed, skip, *tops)
    near = lax.all_to_all(ready, "ctx", 0, 0, axis_index_groups=groups, tiled=True)
    far = lax.ppermute(near, "ctx", core_pairs(n))
    halves = [pltpu.VMEM((TOK, FEATS), BF16)] * 2 + [pltpu.SemaphoreType.DMA((2,))]
    (near_maps,) = call(near_maps_kernel, [((TOK, NS), F32)], 2, 2, halves)(where, *weights[:2], near, first)
    maps, skips = call(far_maps_kernel, [((TOK, 2 * NS), F32), ((QH, NS), F32)], 6)(
        where, *weights[2:], near, far, maps, near_maps
    )
    tp = lax.axis_size("tp")
    swapped = lax.all_to_all(maps.reshape(tp, TOK // tp, 2 * NS), "tp", 0, 0)
    slots = [pltpu.VMEM((TOK, FEATS), F32)] * 2 + [pltpu.SemaphoreType.DMA((4, 2))]
    outs = [((TOK, FEATS), BF16)] * 2 + [((HEADS, TOK), F32)] * 2
    mixed, ginputs, gstep, gdecay = call(cross_kernel, outs, 10, 2, slots)(
        where, within, back, x, g, steps, logs, gains, b, c, near, far, first
    )
    reduced = jnp.sum(swapped, axis=0)
    skip_total = skips[:, ::32].T.reshape(HEADS)
    factor = 1.0 / math.sqrt(lax.axis_size("dp") * TOK * n * PH)
    return (
        mixed[None],
        ginputs[None],
        gstep[None],
        gdecay[None],
        reduced[None, :, :NS],
        reduced[None, :, NS:],
        skip_total * factor,
    )


def solution(mesh):
    in_specs = (
        P("dp", "ctx", "tp"),
        P("dp", "ctx", "tp"),
        P("dp", "ctx", None),
        P("dp", "ctx", None),
        P("dp", "tp", "ctx"),
        P("dp", "tp", "ctx"),
        P("tp"),
    )
    out_specs = (
        P("dp", "ctx", "tp"),
        P("dp", "ctx", "tp"),
        P("dp", "tp", "ctx"),
        P("dp", "tp", "ctx"),
        P("dp", ("ctx", "tp"), None),
        P("dp", ("ctx", "tp"), None),
        P("tp"),
    )
    return jax.shard_map(shards, mesh=mesh, in_specs=in_specs, out_specs=out_specs, check_vma=False)
```
